32 devices in a mesh: parts: 2 (over x), gz: 8 (over z, y), gx: 2 (over core).
Axes of the slice: x: 2, y: 2, z: 4, core: 2. Of those that a mesh axis runs over, the one named last changes fastest.
Arguments:
- noise: float32 [512, 2, 16, 2048], P(('parts', 'gz'), None, None, 'gx'), parts along dimension 0, may hold values from -6 to 6
- scale_index: int32 [512, 2], P(('parts', 'gz')), parts along dimension 0, may hold values from 0 to 15
- rates: float32 [16], replicated, may hold values from 0.000390625 to 0.5
- facies_code: int32 [32, 2048], P('parts', 'gx'), parts along dimension 0, may hold values from 0 to 7
- thresholds: float32 [8], replicated, may hold values from -1 to 1
Outputs:
- latent: float32 [512, 2, 16, 2048], P(('parts', 'gz'), None, None, 'gx'), parts along dimension 0
- facies_soft: float32 [512, 16, 2048], P(('parts', 'gz'), None, 'gx'), parts along dimension 0
The draws below stay inside these ranges and needn't reach their ends.
There are 2 independent parts, one for each index of `parts`. The reference program is written for one: setup_inputs(seed, part) draws one part's arguments, and reference() takes and returns one part's arrays. A program takes and returns all parts, laid end to end along the dimension named above; an argument that names none is the same for every part. Nothing has to cross between parts.
All inputs are finite; a program needn't handle non-finite values.
Results may differ from the reference program's by a relative error of at most 0.00021.
Values sent between devices are 32-bit elements; how exact they have to be, the bound alone decides.
No kernel may reach another device: no remote copies, remote signals or barrier semaphores. Data moves between devices by JAX's collectives and lax.ppermute only.
A program may use at most 64 MiB of HBM per device.

```python
import jax
import jax.numpy as jnp
from jax import lax

YS = 16
NX = 2048
RATE_TABLE_SIZE = 16
NCODE = 8
SWEEPS = 4
DEPTH_LEVELS = 256


def draw_rates(key, part):
    facies_unit = jax.random.uniform(key, (RATE_TABLE_SIZE,), jnp.float32)
    table_entry = jnp.arange(RATE_TABLE_SIZE, dtype=jnp.int32)
    slow_low = 0.1 / DEPTH_LEVELS
    gradual_field = slow_low * jnp.exp(facies_unit * jnp.log(20.0))
    rapid_field = 0.02 * jnp.exp(facies_unit * jnp.log(2.0))
    rapid_group = 0.22 + 0.28 * facies_unit
    return jnp.where(table_entry < RATE_TABLE_SIZE // 2, gradual_field, jnp.where(table_entry < RATE_TABLE_SIZE - 2, rapid_field, rapid_group)).astype(jnp.float32)


def draw_scale_index(key, part):
    random_keys = jax.random.split(key, 6)
    slow_field = jax.random.randint(random_keys[0], (), 0, 2)
    gradual_choice = jax.random.randint(random_keys[1], (DEPTH_LEVELS,), 0, RATE_TABLE_SIZE // 2)
    other_slow = jax.random.randint(random_keys[2], (DEPTH_LEVELS,), 0, RATE_TABLE_SIZE // 2)
    quick_pick = jax.random.randint(random_keys[3], (DEPTH_LEVELS,), RATE_TABLE_SIZE // 2, RATE_TABLE_SIZE - 2)
    which = jax.random.randint(random_keys[4], (DEPTH_LEVELS,), 0, 4)
    mixed = jnp.where(which == 0, other_slow, quick_pick)
    rapid_group_levels = jax.random.randint(random_keys[5], (2,), 0, DEPTH_LEVELS)
    depth_level = jnp.arange(DEPTH_LEVELS, dtype=jnp.int32)
    gradual_column = jnp.where(depth_level == rapid_group_levels[1], RATE_TABLE_SIZE - 2, gradual_choice)
    gradual_column = jnp.where(depth_level == rapid_group_levels[0], RATE_TABLE_SIZE - 1, gradual_column)
    first = jnp.where(slow_field == 0, gradual_column, mixed)
    second = jnp.where(slow_field == 0, mixed, gradual_column)
    return jnp.stack([first, second], axis=1).astype(jnp.int32)


def with_ends(array, rng, least, high):
    longest = array.shape.index(max(array.shape))
    spots = []
    for shift in (0, 1):
        where = [jax.random.randint(jax.random.fold_in(rng, axis), (), 0, length) for axis, length in enumerate(array.shape)]
        where[longest] = (where[longest] + shift) % array.shape[longest]
        spots.append(tuple(where))
    return array.at[spots[0]].set(least).at[spots[1]].set(high)


def levels(stream_key, shape, cuts, low, top_value):
    gain, own = 1.0, jax.random.fold_in(stream_key, 6)
    for position, parts in cuts:
        heights = jnp.exp(jax.random.uniform(jax.random.fold_in(own, position), (parts,), jnp.float32, low / len(cuts), top_value / len(cuts)))
        gain = gain * jnp.repeat(heights, shape[position] // parts).reshape([-1 if axis == position else 1 for axis in range(len(shape))])
    return gain


def scatter_about(key, extent, scale, most, shards=(), kind=jnp.bfloat16):
    loudness = levels(key, extent, shards, -0.22, 0.18) if shards else 1.0
    values = jax.random.normal(key, extent, jnp.float32) * scale * loudness
    return jnp.minimum(jnp.maximum(values, -most), most).astype(kind)


def setup_inputs(seed: int = 0, part: int = 0) -> dict:
    streams_of = jax.random.split(jax.random.key(seed), 6)
    own_keys = jax.random.split(jax.random.fold_in(streams_of[5], part), 6)
    noise = scatter_about(own_keys[0], (DEPTH_LEVELS, 2, YS, NX), 1.0, 6.0, ((0, 8), (3, 2)), jnp.float32)
    scale_index = draw_scale_index(jax.random.fold_in(jax.random.fold_in(streams_of[5], part), 71), part)
    rates = draw_rates(jax.random.fold_in(streams_of[5], 71), part)
    facies_code = with_ends(jax.random.randint(own_keys[3], (YS, NX), 0, NCODE), jax.random.fold_in(own_keys[3], 1), 0, NCODE - 1).astype(jnp.int32)
    thresholds = jnp.clip(jax.random.uniform(streams_of[4], (NCODE,), jnp.float32, -1.0, 1.0), -1.0, 1.0)
    return {"noise": noise, "scale_index": scale_index, "rates": rates, "facies_code": facies_code, "thresholds": thresholds}


def lookup(codes, table):
    slots = jnp.arange(table.shape[0], dtype=jnp.int32)
    hits = (codes[..., None] == slots).astype(jnp.float32)
    return lax.optimization_barrier(jnp.sum(hits * table, axis=-1))

def diffuse(field):
    for sweep in range(SWEEPS):
        padded = jnp.pad(field, ((0, 0), (0, 0), (1, 1), (1, 1)))
        lap = padded[:, :, 1:-1, 2:] + padded[:, :, 1:-1, :-2] + padded[:, :, 2:, 1:-1] + padded[:, :, :-2, 1:-1] - 4.0 * field
        field = field + 0.2 * lap
    return field

def reference(noise, scale_index, rates, facies_code, thresholds):
    alpha = jnp.exp(-lookup(scale_index, rates))
    fwd_gain = jnp.sqrt(1.0 - alpha * alpha)
    bwd_gain = 1.0 - alpha

    def forward(state, inputs):
        level_alpha, level_gain, level_noise = inputs
        state = level_alpha[:, None, None] * state + level_gain[:, None, None] * level_noise
        return (state, state)
    start = jnp.zeros(noise.shape[1:], jnp.float32)
    _, filtered = lax.scan(forward, start, (alpha, fwd_gain, noise))

    def backward(state, inputs):
        level_alpha, level_gain, level_field = inputs
        state = level_alpha[:, None, None] * state + level_gain[:, None, None] * level_field
        return (state, state)
    _, smoothed = lax.scan(backward, start, (alpha, bwd_gain, filtered), reverse=True)
    latent = diffuse(smoothed)
    depth_level = lookup(facies_code, thresholds)
    facies_soft = jax.nn.sigmoid(3.0 * (latent[:, 0] - depth_level[None])) * jax.nn.sigmoid(3.0 * latent[:, 1])
    return (latent, facies_soft)
```

```python
import functools

import jax
import jax.numpy as jnp
from jax import lax
from jax.experimental import pallas as pl
from jax.experimental.pallas import tpu as pltpu
from jax.sharding import PartitionSpec as P

SWEEPS = 4
GROUP = 4
TILE = 128
EDGE = SWEEPS
F32 = jnp.float32
SMEM = pl.BlockSpec(memory_space=pltpu.SMEM)
ANY = pl.BlockSpec(memory_space=pl.ANY)
VMEM = pl.BlockSpec(memory_space=pltpu.VMEM)
HBM = pl.BlockSpec(memory_space=pltpu.HBM)


def splat(value):
    return jnp.full((8, TILE), value, F32)


def row(ref, *at):
    return jnp.broadcast_to(ref[(*at[:-1], pl.ds(at[-1], 1), slice(None))], (8, TILE))


def fill_tables(rates_ref, table):
    for i in range(rates_ref.shape[0]):
        alpha = jnp.exp(-splat(rates_ref[i]))
        table[0, i] = alpha
        table[1, i] = jnp.sqrt(1.0 - alpha * alpha)


def position():
    return lax.rem(lax.axis_index("gz"), GROUP)


def carries(idx_hbm, rates_hbm, noise_hbm, out0, out1, out2, out3, coef, packed, table, pre, wts, tiled, idx, rates, sems):
    outs = (out0, out1, out2, out3)
    levels, columns = noise_hbm.shape[0], noise_hbm.shape[3]
    pos = position()
    core = lax.axis_index("gx")
    small = [
        pltpu.make_async_copy(idx_hbm, idx, sems.at[GROUP, 0]),
        pltpu.make_async_copy(rates_hbm, rates, sems.at[GROUP, 1]),
    ]
    for copy in small:
        copy.start()
    order = (1, 2, 3, 0)
    copies = {}
    for k in order:
        s = pos ^ k
        rows = pl.ds(pl.multiple_of(8 * (s % 2), 8), 8)
        copies[k] = []
        for t in range(columns // TILE):
            source = noise_hbm.at[:, s // 2, rows, pl.ds(t * TILE, TILE)]
            copies[k].append(pltpu.make_async_copy(source, tiled.at[s // 2, t, :, rows, :], sems.at[k, t]))
            copies[k][t].start()
    for copy in small:
        copy.wait()
    fill_tables(rates, table)
    for field in range(2):
        run = splat(1.0)
        for k in range(levels):
            pre[k] = run
            run = run * table[0, idx[field, k]]
        total = run
        post, gather, after = splat(1.0), splat(0.0), splat(0.0)
        for k in reversed(range(levels)):
            alpha, gain = table[0, idx[field, k]], table[1, idx[field, k]]
            coef[0, field, k : k + 1, :] = alpha[:1]
            coef[1, field, k : k + 1, :] = gain[:1]
            gather = pre[k] * (1.0 - alpha) + after * gather
            wts[0, field, k] = gain * post
            wts[1, field, k] = gain * gather
            post = post * alpha
            after = alpha
        wts[0, field, levels] = total
        wts[1, field, levels] = after * gather
    tiles = columns // TILE
    near = (1 - core) * (tiles - 1)
    slots = TILE // EDGE
    slot = lax.rem(lax.broadcasted_iota(jnp.int32, (8, TILE), 1) // EDGE + (1 - core), slots)
    for k in order:
        for copy in copies[k]:
            copy.wait()
        s = pos ^ k
        field = s // 2
        rows = pl.ds(pl.multiple_of(8 * (s % 2), 8), 8)
        for half in range(2):
            ours = range(half * tiles // 2, (half + 1) * tiles // 2)

            def body(level, sums, field=field, rows=rows, ours=ours):
                fwd, bwd = wts[0, field, level], wts[1, field, level]
                new = []
                for t, (one, two) in zip(ours, sums):
                    value = tiled[field, t, level, rows, :]
                    new.append((one + fwd * value, two + bwd * value))
                return tuple(new)

            sums = lax.fori_loop(0, levels, body, ((splat(0.0), splat(0.0)),) * len(ours), unroll=8)
            for t, (one, two) in zip(ours, sums):
                outs[k][0, :, t * TILE : (t + 1) * TILE] = one
                outs[k][1, :, t * TILE : (t + 1) * TILE] = two
        outs[k][0, :, columns:] = wts[0, field, levels]
        outs[k][1, :, columns:] = wts[1, field, levels]
        for first in range(0, levels, slots):
            edge = splat(0.0)
            for level in range(first, min(levels, first + slots)):
                turned = pltpu.roll(tiled[field, near, level, rows, :], EDGE * (level - first), 1)
                edge = jnp.where(slot == level - first, turned, edge)
            packed[first // slots, field, s % 2] = edge


def scan_group(held, lanes, f_in, r_in):
    columns = held.shape[3] - TILE
    f = [f_in]
    for j in range(GROUP):
        f.append(held[j, 0, :, columns:] * f[j] + held[j, 0, :, lanes])
    r = [None] * GROUP + [r_in]
    for j in reversed(range(GROUP)):
        r[j] = held[j, 1, :, lanes] + held[j, 1, :, columns:] * f[j] + held[j, 0, :, columns:] * r[j + 1]
    return f, r


def hold(refs, held):
    pos = position()
    for k, ref in enumerate(refs):
        held[pos ^ k] = ref[...]


def group_total(m0, m1, m2, m3, after, out, held):
    hold((m0, m1, m2, m3), held)
    columns = held.shape[3] - TILE
    zero = splat(0.0)
    for t in range(columns // TILE):
        lanes = slice(t * TILE, (t + 1) * TILE)
        f, r = scan_group(held, lanes, zero, zero)
        out[0, :, lanes] = f[GROUP]
        out[1, :, lanes] = r[0]
    run, factor = splat(1.0), splat(0.0)
    for j in range(GROUP):
        run = run * held[j, 0, :, columns:]
    for j in reversed(range(GROUP)):
        a, c = held[j, 0, :, columns:], held[j, 1, :, columns:]
        factor = c + a * a * factor
    out[0, :, columns:] = run
    out[1, :, columns:] = factor


def enter_group(m0, m1, m2, m3, entering, after, out0, out1, out2, out3, held):
    hold((m0, m1, m2, m3), held)
    columns = held.shape[3] - TILE
    outs = (out0, out1, out2, out3)
    pos = position()
    for t in range(columns // TILE):
        lanes = slice(t * TILE, (t + 1) * TILE)
        f, r = scan_group(held, lanes, entering[0, :, lanes], entering[1, :, lanes])
        for j in range(GROUP):
            held[j, 0, :, lanes] = f[j]
            held[j, 1, :, lanes] = r[j + 1]
    for k in range(GROUP):
        outs[k][...] = held[pos ^ k, :, :, :columns]


def row_neighbours(top, bottom):
    row = lax.broadcasted_iota(jnp.int32, top.shape, 0)
    first, last = row == 0, row == 7
    down_t, down_b = pltpu.roll(top, 1, 0), pltpu.roll(bottom, 1, 0)
    up_t, up_b = pltpu.roll(top, 7, 0), pltpu.roll(bottom, 7, 0)
    return (
        jnp.where(first, 0.0, down_t) + jnp.where(last, up_b, up_t),
        jnp.where(first, down_t, down_b) + jnp.where(last, 0.0, up_b),
    )


def diffuse(top, bottom, keep):
    width = top.shape[1]

    def masked(value):
        return jnp.concatenate([value[:, : width - TILE], value[:, width - TILE :] * keep], axis=1)

    for _ in range(SWEEPS):
        top, bottom = masked(top), masked(bottom)
        over_t, over_b = row_neighbours(top, bottom)
        top = top + over_t + (pltpu.roll(top, 1, 1) + pltpu.roll(top, width - 1, 1))
        bottom = bottom + over_b + (pltpu.roll(bottom, 1, 1) + pltpu.roll(bottom, width - 1, 1))
    return top, bottom


def edge_mask():
    lane = lax.broadcasted_iota(jnp.int32, (8, TILE), 1)
    core = lax.axis_index("gx")
    return ((lane < TILE // 2) == (core == 0)).astype(F32)


def prepare(coef, codes, thresholds, after, reach, bias, pre):
    levels = coef.shape[2]
    for field in range(2):
        run = splat(1.0)
        for k in range(levels):
            run = run * row(coef, 0, field, k)
            pre[k] = run
        down, up = splat(0.0), splat(1.0)
        for k in reversed(range(levels)):
            alpha = row(coef, 0, field, k)
            down = alpha * down + (1.0 - alpha) * pre[k]
            up = alpha * up
            reach[0, field, k : k + 1, :] = down[:1]
            reach[1, field, k : k + 1, :] = up[:1]
    code = codes[...]
    value = jnp.zeros(code.shape, F32)
    for i in range(thresholds.shape[0]):
        value = jnp.where(code == i, thresholds[i], value)
    bias[...] = value


def local_field(field, coef, packed, noise_hbm, after, out, buf, work, sems):
    levels, _, ys, columns = noise_hbm.shape
    tiles = columns // TILE

    def fetch_group(turn, go):
        at = pl.ds(pl.multiple_of(turn * 8, 8), 8)
        for t in range(tiles):
            source = noise_hbm.at[at, field, :, pl.ds(t * TILE, TILE)]
            copy = pltpu.make_async_copy(source, buf.at[t, at], sems.at[turn, t])
            if go:
                copy.start()
            else:
                copy.wait()

    for turn in range(levels // 8):
        fetch_group(turn, True)
    core = lax.axis_index("gx")
    lane = lax.broadcasted_iota(jnp.int32, (8, TILE), 1)
    keep = edge_mask()
    sent = jnp.where(core == 0, lane, TILE - 1 - lane) < EDGE
    slots = TILE // EDGE
    for level in range(levels):
        for top in range(2):
            edge = packed[level // slots, field, top]
            edge = pltpu.roll(edge, (TILE - EDGE * (level % slots)) % TILE, 1)
            buf[tiles, level, 8 * top : 8 * top + 8, :] = jnp.where(sent, edge, 0.0)
    flat = buf.reshape(tiles + 1, levels * ys, TILE)
    first, last = lane == 0, lane == TILE - 1

    def sweep(get, put, all_tiles):
        above = [splat(0.0)] * (tiles + 1)
        here = get(0)
        for y in range(ys):
            below = get(y + 1) if y + 1 < ys else [splat(0.0)] * (tiles + 1)
            right = [pltpu.roll(v, TILE - 1, 1) for v in here]
            left = [pltpu.roll(v, 1, 1) for v in here]
            new = []
            for t in range(tiles + all_tiles):
                beside = jnp.where(first, left[t - 1], left[t])
                beside += jnp.where(last, right[(t + 1) % (tiles + 1)], right[t])
                new.append(here[t] + beside + (above[t] + below[t]))
            if all_tiles:
                new[tiles] = new[tiles] * keep
            put(y, new)
            above, here = here, below

    def group(turn, _):
        fetch_group(turn, False)
        base = turn * 8 * ys

        def fetch(y):
            at = pl.ds(base + y, 8, stride=ys)
            return [flat[t, at, :] for t in range(tiles + 1)]

        def give(y, new):
            for t, value in enumerate(new):
                flat[t, pl.ds(base + y, 8, stride=ys), :] = value

        def saver(slot):
            def put(y, new):
                for t, value in enumerate(new):
                    work[slot, t, y] = value

            return put

        def loader(slot):
            return lambda y: [work[slot, t, y] for t in range(tiles + 1)]

        get = fetch
        for turn in range(SWEEPS - 1):
            sweep(get, saver(turn % 2), True)
            get = loader(turn % 2)
        sweep(get, give, False)
        return 0

    lax.fori_loop(0, levels // 8, group, 0)
    scale = 0.2**SWEEPS
    spots = [(t, top) for t in range(tiles) for top in range(ys // 8)]

    def forward(level, state):
        alpha, gain = row(coef, 0, field, level), row(coef, 1, field, level) * scale
        new = []
        for (t, top), old in zip(spots, state):
            value = alpha * old + gain * buf[t, level, 8 * top : 8 * top + 8, :]
            buf[t, level, 8 * top : 8 * top + 8, :] = value
            new.append(value)
        return tuple(new)

    def backward(turn, state):
        level = levels - 1 - turn
        alpha = row(coef, 0, field, level)
        gain = 1.0 - alpha
        new = []
        for (t, top), old in zip(spots, state):
            value = alpha * old + gain * buf[t, level, 8 * top : 8 * top + 8, :]
            out[level, 8 * top : 8 * top + 8, t * TILE : (t + 1) * TILE] = value
            new.append(value)
        return tuple(new)

    zeros = (splat(0.0),) * len(spots)
    lax.fori_loop(0, levels, forward, zeros, unroll=2)
    lax.fori_loop(0, levels, backward, zeros, unroll=2)


def edges(m0, m1, m2, m3, after, out):
    columns = m0.shape[2]
    near = pl.ds(pl.multiple_of((1 - lax.axis_index("gx")) * (columns - TILE), TILE), TILE)
    for k, ref in enumerate((m0, m1, m2, m3)):
        out[k] = ref[:, :, near]


def finish(g0, g1, reach, bias, m0, m1, m2, m3, halo, latent_hbm, soft_hbm, state, latent, soft, sems):
    levels, columns = g0.shape[0], g0.shape[2]
    pos = position()
    for k, ref in enumerate((m0, m1, m2, m3)):
        s = pos ^ k
        rows = pl.ds(pl.multiple_of(8 * (s % 2), 8), 8)
        for kind in range(2):
            state[kind, s // 2, rows, :columns] = ref[kind]
            state[kind, s // 2, rows, columns:] = halo[k, kind]
    keep = edge_mask()
    for kind in range(2):
        for field in range(2):
            top, bottom = diffuse(state[kind, field, 0:8, :], state[kind, field, 8:16, :], keep)
            state[kind, field, 0:8, :] = top * 0.2**SWEEPS
            state[kind, field, 8:16, :] = bottom * 0.2**SWEEPS
    parts = sems.shape[0]
    step = levels // parts
    tiles = columns // TILE
    copies = []
    for i in range(parts):

        def body(turn, _, i=i):
            rows = pl.ds(pl.multiple_of(8 * (turn // tiles), 8), 8)
            lanes = pl.ds(pl.multiple_of(TILE * lax.rem(turn, tiles), TILE), TILE)
            f = [state[0, field, rows, lanes] for field in range(2)]
            r = [state[1, field, rows, lanes] for field in range(2)]
            base = bias[rows, lanes]
            for level in range(i * step, (i + 1) * step):
                one = g0[level, rows, lanes] + row(reach, 0, 0, level) * f[0] + row(reach, 1, 0, level) * r[0]
                two = g1[level, rows, lanes] + row(reach, 0, 1, level) * f[1] + row(reach, 1, 1, level) * r[1]
                latent[level, 0, rows, lanes] = one
                latent[level, 1, rows, lanes] = two
                half = 0.5 + 0.5 * jnp.tanh(1.5 * (one - base))
                soft[level, rows, lanes] = half * (0.5 + 0.5 * jnp.tanh(1.5 * two))
            return 0

        lax.fori_loop(0, 2 * tiles, body, 0)
        at = pl.ds(i * step, step)
        copies += [
            pltpu.make_async_copy(latent.at[at], latent_hbm.at[at], sems.at[i, 0]),
            pltpu.make_async_copy(soft.at[at], soft_hbm.at[at], sems.at[i, 1]),
        ]
        for copy in copies[-2:]:
            copy.start()
    for copy in copies:
        copy.wait()


def params(mib):
    return pltpu.CompilerParams(vmem_limit_bytes=mib << 20)


def cost(flops, data):
    return pl.CostEstimate(flops=flops, bytes_accessed=data, transcendentals=0)


def xor_permute(value, axis, by):
    return lax.ppermute(value, axis, [(i, i ^ by) for i in range(lax.axis_size(axis))])


def entering_states(total, groups):
    columns = total.shape[2] - TILE
    group = lax.axis_index("gz") // GROUP

    def wide(value):
        return jnp.tile(value, (1, columns // TILE))

    def fwd(t):
        return t[0, :, :columns]

    def bwd(t):
        return t[1, :, :columns]

    if groups == 2:
        sent = jnp.where(group == 0, jnp.concatenate([total[0, :, :columns], total[0, :, columns:]], axis=1),
                         total[1])
        got = xor_permute(sent, "gz", GROUP)
        zero = jnp.zeros((8, columns), F32)
        below = got[:, :columns] + wide(got[:, columns:]) * fwd(total)
        return jnp.stack([jnp.where(group == 0, zero, got[:, :columns]), jnp.where(group == 0, below, zero)])
    size = GROUP * groups
    totals = [total]
    for turn in range(1, groups):
        totals.append(lax.ppermute(total, "gz", [(i, (i + GROUP * turn) % size) for i in range(size)]))
    stacked = jnp.stack(totals)
    state = jnp.zeros((8, columns), F32)
    f = [state]
    at = [lax.dynamic_index_in_dim(stacked, (group - j) % groups, keepdims=False) for j in range(groups)]
    for j in range(groups):
        state = wide(at[j][0, :, columns:]) * state + fwd(at[j])
        f.append(state)
    state = jnp.zeros((8, columns), F32)
    r = [None] * groups + [state]
    for j in reversed(range(groups)):
        state = bwd(at[j]) + wide(at[j][1, :, columns:]) * f[j] + wide(at[j][0, :, columns:]) * state
        r[j] = state
    return jnp.stack(
        [
            lax.dynamic_index_in_dim(jnp.stack(f[:groups]), group, keepdims=False),
            lax.dynamic_index_in_dim(jnp.stack(r[1:]), group, keepdims=False),
        ]
    )


def shards(noise, scale_index, rates, facies_code, thresholds):
    levels, _, ys, columns = noise.shape
    assert ys == 16 and columns % (2 * TILE) == 0 and levels % 8 == 0
    tiles = columns // TILE
    groups = lax.axis_size("gz") // GROUP
    message = jax.ShapeDtypeStruct((2, 8, columns + TILE), F32)
    folds = -(-levels * EDGE // TILE)
    *mine, coef, packed = pl.pallas_call(
        carries,
        out_shape=[message] * GROUP
        + [
            jax.ShapeDtypeStruct((2, 2, levels, TILE), F32),
            jax.ShapeDtypeStruct((folds, 2, 2, 8, TILE), F32),
        ],
        in_specs=[HBM, HBM, HBM],
        out_specs=[VMEM] * (GROUP + 2),
        scratch_shapes=[
            pltpu.VMEM((2, rates.shape[0], 8, TILE), F32),
            pltpu.VMEM((levels, 8, TILE), F32),
            pltpu.VMEM((2, 2, levels + 1, 8, TILE), F32),
            pltpu.VMEM((2, tiles, levels, ys, TILE), F32),
            pltpu.SMEM((2, levels), jnp.int32),
            pltpu.SMEM(rates.shape, F32),
            pltpu.SemaphoreType.DMA((GROUP + 1, tiles)),
        ],
        compiler_params=params(52),
        cost_estimate=cost(4 * noise.size, 4 * noise.size),
        name="carries",
    )(scale_index.T, rates, noise)
    got = [mine[0]] + [xor_permute(mine[k], "gz", k) for k in range(1, GROUP)]
    halo = xor_permute(packed, "gx", 1)

    def local(field, after):
        return pl.pallas_call(
            functools.partial(local_field, field),
            out_shape=jax.ShapeDtypeStruct((levels, ys, columns), F32),
            in_specs=[VMEM, VMEM, HBM, ANY],
            out_specs=VMEM,
            scratch_shapes=[
                pltpu.VMEM((tiles + 1, levels, ys, TILE), F32),
                pltpu.VMEM((2, tiles + 1, ys, 8, TILE), F32),
                pltpu.SemaphoreType.DMA((levels // 8, tiles)),
            ],
            compiler_params=params(50),
            cost_estimate=cost(80 * noise.size // 2, 4 * noise.size),
            name=f"local{field}",
        )(coef, halo, noise, after)

    local0 = local(0, halo)
    held = pltpu.VMEM((GROUP, 2, 8, columns + TILE), F32)
    total = pl.pallas_call(
        group_total,
        out_shape=message,
        in_specs=[VMEM] * GROUP + [ANY],
        out_specs=VMEM,
        scratch_shapes=[held],
        compiler_params=params(8),
        name="group_total",
    )(*got, local0)
    reach, bias = pl.pallas_call(
        prepare,
        out_shape=[
            jax.ShapeDtypeStruct((2, 2, levels, TILE), F32),
            jax.ShapeDtypeStruct((ys, columns), F32),
        ],
        in_specs=[VMEM, VMEM, SMEM, ANY],
        out_specs=[VMEM] * 2,
        scratch_shapes=[pltpu.VMEM((levels, 8, TILE), F32)],
        compiler_params=params(4),
        cost_estimate=cost(noise.size, noise.size),
        name="prepare",
    )(coef, facies_code, thresholds, total)
    entering = entering_states(total, groups)
    state = jax.ShapeDtypeStruct((2, 8, columns), F32)
    own = pl.pallas_call(
        enter_group,
        out_shape=[state] * GROUP,
        in_specs=[VMEM] * (GROUP + 1) + [ANY],
        out_specs=[VMEM] * GROUP,
        scratch_shapes=[held],
        compiler_params=params(8),
        name="enter_group",
    )(*got, entering, reach)
    states = [own[0]] + [xor_permute(own[k], "gz", k) for k in range(1, GROUP)]
    local1 = local(1, own[0])
    near = pl.pallas_call(
        edges,
        out_shape=jax.ShapeDtypeStruct((GROUP, 2, 8, TILE), F32),
        in_specs=[VMEM] * GROUP + [ANY],
        out_specs=VMEM,
        compiler_params=params(4),
        name="edges",
    )(*states, local1)
    near = xor_permute(near, "gx", 1)
    out = [
        jax.ShapeDtypeStruct(noise.shape, F32),
        jax.ShapeDtypeStruct((levels, ys, columns), F32),
    ]
    latent, soft = pl.pallas_call(
        finish,
        out_shape=out,
        in_specs=[VMEM] * 9,
        out_specs=[ANY, ANY],
        scratch_shapes=[
            pltpu.VMEM((2, 2, ys, columns + TILE), F32),
            pltpu.VMEM(noise.shape, F32),
            pltpu.VMEM((levels, ys, columns), F32),
            pltpu.SemaphoreType.DMA((4, 2)),
        ],
        compiler_params=params(24),
        name="finish",
    )(local0, local1, reach, bias, *states, near)
    return latent, soft


def solution(mesh):
    return jax.shard_map(
        shards,
        mesh=mesh,
        in_specs=(
            P(("parts", "gz"), None, None, "gx"),
            P(("parts", "gz"), None),
            P(),
            P("parts", "gx"),
            P(),
        ),
        out_specs=(P(("parts", "gz"), None, None, "gx"), P(("parts", "gz"), None, "gx")),
        check_vma=False,
    )
```

```python
import functools

import jax
import jax.numpy as jnp
from jax import lax
from jax.experimental import pallas as pl
from jax.experimental.pallas import tpu as pltpu
from jax.sharding import PartitionSpec as P

SWEEPS = 4
GROUP = 4
TILE = 128
F32 = jnp.float32
SMEM = pl.BlockSpec(memory_space=pltpu.SMEM)
ANY = pl.BlockSpec(memory_space=pl.ANY)
VMEM = pl.BlockSpec(memory_space=pltpu.VMEM)
HBM = pl.BlockSpec(memory_space=pltpu.HBM)


def splat(value):
    return jnp.full((8, TILE), value, F32)


def row(ref, *at):
    return jnp.broadcast_to(ref[(*at[:-1], pl.ds(at[-1], 1), slice(None))], (8, TILE))


def coefficients(scale_index, rates):
    slots = jnp.arange(rates.shape[0], dtype=jnp.int32)
    hits = (scale_index.T[..., None] == slots).astype(F32)
    alpha = jnp.exp(-jnp.sum(hits * rates, axis=-1))
    both = jnp.stack([alpha, jnp.sqrt(1.0 - alpha * alpha)])
    return jnp.broadcast_to(both[..., None], (*both.shape, TILE))


def position():
    return lax.rem(lax.axis_index("gz"), GROUP)


def carries(coef, noise_hbm, out0, out1, out2, out3, packed, tiled0, tiled1, held, pre, wts, sems):
    outs, tiled = (out0, out1, out2, out3), (tiled0, tiled1)
    levels, columns = noise_hbm.shape[0], noise_hbm.shape[3]
    tiles = columns // TILE
    pos = position()
    core = lax.axis_index("gx")
    copies = []
    for s in range(GROUP):
        rows = slice(8 * (s % 2), 8 * (s % 2) + 8)
        copies.append([])
        for t in range(tiles):
            source = noise_hbm.at[:, s // 2, rows, pl.ds(t * TILE, TILE)]
            copies[s].append(pltpu.make_async_copy(source, tiled[s // 2].at[t, :, rows, :], sems.at[s, t]))
            copies[s][t].start()
    for field in range(2):
        run = splat(1.0)
        for k in range(levels):
            pre[k] = run
            run = run * row(coef, 0, field, k)
        total = run
        post, gather, after = splat(1.0), splat(0.0), splat(0.0)
        for k in reversed(range(levels)):
            alpha, gain = row(coef, 0, field, k), row(coef, 1, field, k)
            gather = pre[k] * (1.0 - alpha) + after * gather
            wts[0, field, k] = gain * post
            wts[1, field, k] = gain * gather
            post = post * alpha
            after = alpha
        wts[0, field, levels] = total
        wts[1, field, levels] = after * gather
    near = (1 - core) * (tiles - 1)
    for s in range(GROUP):
        for copy in copies[s]:
            copy.wait()
        field, k = s // 2, pos ^ s
        rows = slice(8 * (s % 2), 8 * (s % 2) + 8)
        for half in range(2):
            ours = range(half * tiles // 2, (half + 1) * tiles // 2)

            def body(level, sums, field=field, rows=rows, ours=ours):
                fwd, bwd = wts[0, field, level], wts[1, field, level]
                new = []
                for t, (one, two) in zip(ours, sums):
                    value = tiled[field][t, level, rows, :]
                    new.append((one + fwd * value, two + bwd * value))
                return tuple(new)

            sums = lax.fori_loop(0, levels, body, ((splat(0.0), splat(0.0)),) * len(ours), unroll=True)
            for t, (one, two) in zip(ours, sums):
                held[k, 0, :, t * TILE : (t + 1) * TILE] = one
                held[k, 1, :, t * TILE : (t + 1) * TILE] = two
        held[k, 0, :, columns:] = wts[0, field, levels]
        held[k, 1, :, columns:] = wts[1, field, levels]
    for k in range(GROUP):
        outs[k][...] = held[k]
    for field in range(2):
        flat = tiled[field].reshape(tiles, levels * 16, TILE)
        for first in range(0, 16, TILE // levels):
            rows = [
                flat[near, pl.ds(8 * g * 16 + y, 8, stride=16), :]
                for y in range(first, first + TILE // levels)
                for g in range(levels // 8)
            ]
            turned = jnp.concatenate(rows, axis=0).T
            packed[field, first * levels // TILE] = jnp.where(core == 0, turned[TILE - 8 :], turned[:8])


def scan_group(held, lanes, f_in, r_in):
    columns = held.shape[3] - TILE
    f = [f_in]
    for j in range(GROUP):
        f.append(held[j, 0, :, columns:] * f[j] + held[j, 0, :, lanes])
    r = [None] * GROUP + [r_in]
    for j in reversed(range(GROUP)):
        r[j] = held[j, 1, :, lanes] + held[j, 1, :, columns:] * f[j] + held[j, 0, :, columns:] * r[j + 1]
    return f, r


def hold(refs, held):
    pos = position()
    for k, ref in enumerate(refs):
        held[pos ^ k] = ref[...]


def group_total(m0, m1, m2, m3, after, out, held):
    hold((m0, m1, m2, m3), held)
    columns = held.shape[3] - TILE
    zero = splat(0.0)
    for t in range(columns // TILE):
        lanes = slice(t * TILE, (t + 1) * TILE)
        f, r = scan_group(held, lanes, zero, zero)
        out[0, :, lanes] = f[GROUP]
        out[1, :, lanes] = r[0]
    run, factor = splat(1.0), splat(0.0)
    for j in range(GROUP):
        run = run * held[j, 0, :, columns:]
    for j in reversed(range(GROUP)):
        a, c = held[j, 0, :, columns:], held[j, 1, :, columns:]
        factor = c + a * a * factor
    out[0, :, columns:] = run
    out[1, :, columns:] = factor


def enter_group(m0, m1, m2, m3, entering, after, out0, out1, out2, out3, held):
    hold((m0, m1, m2, m3), held)
    columns = held.shape[3] - TILE
    outs = (out0, out1, out2, out3)
    pos = position()
    for t in range(columns // TILE):
        lanes = slice(t * TILE, (t + 1) * TILE)
        f, r = scan_group(held, lanes, entering[0, :, lanes], entering[1, :, lanes])
        for j in range(GROUP):
            held[j, 0, :, lanes] = f[j]
            held[j, 1, :, lanes] = r[j + 1]
    for k in range(GROUP):
        outs[k][...] = held[pos ^ k, :, :, :columns]


def row_neighbours(top, bottom):
    row = lax.broadcasted_iota(jnp.int32, top.shape, 0)
    first, last = row == 0, row == 7
    down_t, down_b = pltpu.roll(top, 1, 0), pltpu.roll(bottom, 1, 0)
    up_t, up_b = pltpu.roll(top, 7, 0), pltpu.roll(bottom, 7, 0)
    return (
        jnp.where(first, 0.0, down_t) + jnp.where(last, up_b, up_t),
        jnp.where(first, down_t, down_b) + jnp.where(last, 0.0, up_b),
    )


def diffuse(top, bottom, keep):
    width = top.shape[1]

    def masked(value):
        return jnp.concatenate([value[:, : width - TILE], value[:, width - TILE :] * keep], axis=1)

    for _ in range(SWEEPS):
        top, bottom = masked(top), masked(bottom)
        over_t, over_b = row_neighbours(top, bottom)
        top = top + over_t + (pltpu.roll(top, 1, 1) + pltpu.roll(top, width - 1, 1))
        bottom = bottom + over_b + (pltpu.roll(bottom, 1, 1) + pltpu.roll(bottom, width - 1, 1))
    return top, bottom


def edge_mask():
    lane = lax.broadcasted_iota(jnp.int32, (8, TILE), 1)
    core = lax.axis_index("gx")
    return ((lane < TILE // 2) == (core == 0)).astype(F32)


def prepare(coef, codes, thresholds, after, reach, bias, pre):
    levels = coef.shape[2]
    for field in range(2):
        run = splat(1.0)
        for k in range(levels):
            run = run * row(coef, 0, field, k)
            pre[k] = run
        down, up = splat(0.0), splat(1.0)
        for k in reversed(range(levels)):
            alpha = row(coef, 0, field, k)
            down = alpha * down + (1.0 - alpha) * pre[k]
            up = alpha * up
            reach[0, field, k : k + 1, :] = down[:1]
            reach[1, field, k : k + 1, :] = up[:1]
    code = codes[...]
    value = jnp.zeros(code.shape, F32)
    for i in range(thresholds.shape[0]):
        value = jnp.where(code == i, thresholds[i], value)
    bias[...] = value


def local_first(coef, packed, tiled, noise_hbm, out, tiled_next, buf, work, sems):
    copies = [
        pltpu.make_async_copy(noise_hbm.at[:, 1, :, pl.ds(t * TILE, TILE)], tiled_next.at[t], sems.at[t])
        for t in range(tiled.shape[0])
    ]
    for copy in copies:
        copy.start()
    local_field(0, coef, packed, tiled, None, out, buf, work)
    for copy in copies:
        copy.wait()


def local_field(field, coef, packed, tiled, after, out, buf, work):
    tiles, levels, ys, _ = tiled.shape
    columns = tiles * TILE
    ranges = TILE // levels
    span = columns // ranges
    blocks = span // TILE
    main = 16
    core = lax.axis_index("gx")
    lane = lax.broadcasted_iota(jnp.int32, (8, TILE), 1)
    keep_left = (lane >= levels) | (core == 1)
    keep_right = (lane < TILE - levels) | (core == 0)
    source = tiled.reshape(tiles, levels * ys, TILE)
    flat = buf.reshape(tiles, levels * ys, TILE)
    for slot in range(2):
        for y in range(ys):
            work[slot, y, 0:8, :] = splat(0.0)
            work[slot, y, main + span + 8 :, :] = splat(0.0)

    def pieces(y):
        return [(c, g, pl.ds(8 * g * ys + y, 8, stride=ys)) for c in range(ranges) for g in range(levels // 8)]

    for y in range(ys):
        for b in range(blocks):
            rows = [source[c * blocks + b, at, :] for c, g, at in pieces(y)]
            work[0, y, main + b * TILE : main + (b + 1) * TILE, :] = jnp.concatenate(rows, axis=0).T
        edge, place = packed[field, y // ranges], y % ranges
        left = pltpu.roll(work[0, y, main + span - 8 : main + span, :], levels, 1)
        right = pltpu.roll(work[0, y, main : main + 8, :], TILE - levels, 1)
        far_left = pltpu.roll(edge, (TILE - levels * place) % TILE, 1)
        far_right = pltpu.roll(edge, levels * (ranges - 1 - place), 1)
        left = jnp.where(keep_left, jnp.where(lane < levels, far_left, left), 0.0)
        right = jnp.where(keep_right, jnp.where(lane >= TILE - levels, far_right, right), 0.0)
        work[0, y, main - 8 : main, :] = left
        work[0, y, main + span : main + span + 8, :] = right

    def block(src, at, before, later, keep=None):
        above, here = splat(0.0), work[src, 0, at, :]
        for y in range(ys):
            below = work[src, y + 1, at, :] if y + 1 < ys else splat(0.0)
            new = here + (work[src, y, before, :] + work[src, y, later, :]) + (above + below)
            if keep is not None:
                new = jnp.where(keep, new, 0.0)
            work[1 - src, y, at, :] = new
            above, here = here, below

    for turn in range(SWEEPS):
        src = turn % 2

        def step(r, _, src=src):
            at = pl.multiple_of(main + 8 * r, 8)
            block(src, pl.ds(at, 8), pl.ds(at - 1, 8), pl.ds(at + 1, 8))
            return 0

        lax.fori_loop(0, span // 8, step, 0, unroll=True)
        if turn + 1 < SWEEPS:
            for at, keep in ((main - 8, keep_left), (main + span, keep_right)):
                block(src, pl.ds(at, 8), pl.ds(at - 1, 8), pl.ds(at + 1, 8), keep)
    for y in range(ys):
        for b in range(blocks):
            turned = work[SWEEPS % 2, y, main + b * TILE : main + (b + 1) * TILE, :].T
            for i, (c, g, at) in enumerate(pieces(y)):
                flat[c * blocks + b, at, :] = turned[8 * i : 8 * i + 8]
    scale = 0.2**SWEEPS
    spots = [(t, top) for t in range(tiles) for top in range(ys // 8)]

    def forward(level, state):
        alpha, gain = row(coef, 0, field, level), row(coef, 1, field, level) * scale
        new = []
        for (t, top), old in zip(spots, state):
            value = alpha * old + gain * buf[t, level, 8 * top : 8 * top + 8, :]
            buf[t, level, 8 * top : 8 * top + 8, :] = value
            new.append(value)
        return tuple(new)

    def backward(turn, state):
        level = levels - 1 - turn
        alpha = row(coef, 0, field, level)
        gain = 1.0 - alpha
        new = []
        for (t, top), old in zip(spots, state):
            value = alpha * old + gain * buf[t, level, 8 * top : 8 * top + 8, :]
            out[level, 8 * top : 8 * top + 8, t * TILE : (t + 1) * TILE] = value
            new.append(value)
        return tuple(new)

    zeros = (splat(0.0),) * len(spots)
    lax.fori_loop(0, levels, forward, zeros, unroll=True)
    lax.fori_loop(0, levels, backward, zeros, unroll=True)


def edges(m0, m1, m2, m3, after, out):
    columns = m0.shape[2]
    near = pl.ds(pl.multiple_of((1 - lax.axis_index("gx")) * (columns - TILE), TILE), TILE)
    for k, ref in enumerate((m0, m1, m2, m3)):
        out[k] = ref[:, :, near]


def finish(g0, g1, reach, bias, m0, m1, m2, m3, halo, latent_hbm, soft_hbm, state, latent, soft, sems):
    levels, columns = g0.shape[0], g0.shape[2]
    pos = position()
    for k, ref in enumerate((m0, m1, m2, m3)):
        s = pos ^ k
        rows = pl.ds(pl.multiple_of(8 * (s % 2), 8), 8)
        for kind in range(2):
            state[kind, s // 2, rows, :columns] = ref[kind]
            state[kind, s // 2, rows, columns:] = halo[k, kind]
    keep = edge_mask()
    for kind in range(2):
        for field in range(2):
            top, bottom = diffuse(state[kind, field, 0:8, :], state[kind, field, 8:16, :], keep)
            state[kind, field, 0:8, :] = top * 0.2**SWEEPS
            state[kind, field, 8:16, :] = bottom * 0.2**SWEEPS
    parts = sems.shape[0]
    step = levels // parts
    tiles = columns // TILE
    copies = []
    for i in range(parts):

        def body(turn, _, i=i):
            rows = pl.ds(pl.multiple_of(8 * (turn // tiles), 8), 8)
            lanes = pl.ds(pl.multiple_of(TILE * lax.rem(turn, tiles), TILE), TILE)
            f = [state[0, field, rows, lanes] for field in range(2)]
            r = [state[1, field, rows, lanes] for field in range(2)]
            base = bias[rows, lanes]
            for level in range(i * step, (i + 1) * step):
                one = g0[level, rows, lanes] + row(reach, 0, 0, level) * f[0] + row(reach, 1, 0, level) * r[0]
                two = g1[level, rows, lanes] + row(reach, 0, 1, level) * f[1] + row(reach, 1, 1, level) * r[1]
                latent[level, 0, rows, lanes] = one
                latent[level, 1, rows, lanes] = two
                half = 0.5 + 0.5 * jnp.tanh(1.5 * (one - base))
                soft[level, rows, lanes] = half * (0.5 + 0.5 * jnp.tanh(1.5 * two))
            return 0

        lax.fori_loop(0, 2 * tiles, body, 0, unroll=True)
        at = pl.ds(i * step, step)
        copies += [
            pltpu.make_async_copy(latent.at[at], latent_hbm.at[at], sems.at[i, 0]),
            pltpu.make_async_copy(soft.at[at], soft_hbm.at[at], sems.at[i, 1]),
        ]
        for copy in copies[-2:]:
            copy.start()
    for copy in copies:
        copy.wait()


def params(mib):
    return pltpu.CompilerParams(vmem_limit_bytes=mib << 20)


def cost(flops, data):
    return pl.CostEstimate(flops=flops, bytes_accessed=data, transcendentals=0)


def xor_permute(value, axis, by):
    return lax.ppermute(value, axis, [(i, i ^ by) for i in range(lax.axis_size(axis))])


def entering_states(total, groups):
    columns = total.shape[2] - TILE
    group = lax.axis_index("gz") // GROUP

    def wide(value):
        return jnp.tile(value, (1, columns // TILE))

    def fwd(t):
        return t[0, :, :columns]

    def bwd(t):
        return t[1, :, :columns]

    if groups == 2:
        sent = jnp.where(group == 0, jnp.concatenate([total[0, :, :columns], total[0, :, columns:]], axis=1),
                         total[1])
        got = xor_permute(sent, "gz", GROUP)
        zero = jnp.zeros((8, columns), F32)
        below = got[:, :columns] + wide(got[:, columns:]) * fwd(total)
        return jnp.stack([jnp.where(group == 0, zero, got[:, :columns]), jnp.where(group == 0, below, zero)])
    size = GROUP * groups
    totals = [total]
    for turn in range(1, groups):
        totals.append(lax.ppermute(total, "gz", [(i, (i + GROUP * turn) % size) for i in range(size)]))
    stacked = jnp.stack(totals)
    state = jnp.zeros((8, columns), F32)
    f = [state]
    at = [lax.dynamic_index_in_dim(stacked, (group - j) % groups, keepdims=False) for j in range(groups)]
    for j in range(groups):
        state = wide(at[j][0, :, columns:]) * state + fwd(at[j])
        f.append(state)
    state = jnp.zeros((8, columns), F32)
    r = [None] * groups + [state]
    for j in reversed(range(groups)):
        state = bwd(at[j]) + wide(at[j][1, :, columns:]) * f[j] + wide(at[j][0, :, columns:]) * state
        r[j] = state
    return jnp.stack(
        [
            lax.dynamic_index_in_dim(jnp.stack(f[:groups]), group, keepdims=False),
            lax.dynamic_index_in_dim(jnp.stack(r[1:]), group, keepdims=False),
        ]
    )


def shards(noise, scale_index, rates, facies_code, thresholds):
    levels, _, ys, columns = noise.shape
    assert ys == 16 and levels % 8 == 0 and TILE % levels == 0 and columns * levels % (TILE * TILE) == 0
    tiles = columns // TILE
    groups = lax.axis_size("gz") // GROUP
    message = jax.ShapeDtypeStruct((2, 8, columns + TILE), F32)
    coef = coefficients(scale_index, rates)
    *mine, packed, tiled0 = pl.pallas_call(
        carries,
        out_shape=[message] * GROUP
        + [
            jax.ShapeDtypeStruct((2, ys * levels // TILE, 8, TILE), F32),
            jax.ShapeDtypeStruct((tiles, levels, ys, TILE), F32),
        ],
        in_specs=[VMEM, HBM],
        out_specs=[VMEM] * (GROUP + 2),
        scratch_shapes=[
            pltpu.VMEM((tiles, levels, ys, TILE), F32),
            pltpu.VMEM((GROUP, 2, 8, columns + TILE), F32),
            pltpu.VMEM((levels, 8, TILE), F32),
            pltpu.VMEM((2, 2, levels + 1, 8, TILE), F32),
            pltpu.SemaphoreType.DMA((GROUP, tiles)),
        ],
        compiler_params=params(50),
        cost_estimate=cost(4 * noise.size, 4 * noise.size),
        name="carries",
    )(coef, noise)
    got = [mine[0]] + [xor_permute(mine[k], "gz", k) for k in range(1, GROUP)]
    halo = xor_permute(packed, "gx", 1)

    field_out = jax.ShapeDtypeStruct((levels, ys, columns), F32)
    field_tiled = jax.ShapeDtypeStruct((tiles, levels, ys, TILE), F32)
    scratch = [
        pltpu.VMEM((tiles, levels, ys, TILE), F32),
        pltpu.VMEM((2, ys, columns * levels // TILE + 32, TILE), F32),
    ]
    local0, tiled1 = pl.pallas_call(
        local_first,
        out_shape=[field_out, field_tiled],
        in_specs=[VMEM, VMEM, VMEM, HBM],
        out_specs=[VMEM] * 2,
        scratch_shapes=[*scratch, pltpu.SemaphoreType.DMA((tiles,))],
        compiler_params=params(45),
        cost_estimate=cost(40 * noise.size, 4 * noise.size),
        name="local0",
    )(coef, halo, tiled0, noise)
    held = pltpu.VMEM((GROUP, 2, 8, columns + TILE), F32)
    total = pl.pallas_call(
        group_total,
        out_shape=message,
        in_specs=[VMEM] * GROUP + [ANY],
        out_specs=VMEM,
        scratch_shapes=[held],
        compiler_params=params(8),
        name="group_total",
    )(*got, local0)
    reach, bias = pl.pallas_call(
        prepare,
        out_shape=[
            jax.ShapeDtypeStruct((2, 2, levels, TILE), F32),
            jax.ShapeDtypeStruct((ys, columns), F32),
        ],
        in_specs=[VMEM, VMEM, SMEM, ANY],
        out_specs=[VMEM] * 2,
        scratch_shapes=[pltpu.VMEM((levels, 8, TILE), F32)],
        compiler_params=params(4),
        cost_estimate=cost(noise.size, noise.size),
        name="prepare",
    )(coef, facies_code, thresholds, total)
    entering = entering_states(total, groups)
    state = jax.ShapeDtypeStruct((2, 8, columns), F32)
    own = pl.pallas_call(
        enter_group,
        out_shape=[state] * GROUP,
        in_specs=[VMEM] * (GROUP + 1) + [ANY],
        out_specs=[VMEM] * GROUP,
        scratch_shapes=[held],
        compiler_params=params(8),
        name="enter_group",
    )(*got, entering, reach)
    states = [own[0]] + [xor_permute(own[k], "gz", k) for k in range(1, GROUP)]
    local1 = pl.pallas_call(
        functools.partial(local_field, 1),
        out_shape=field_out,
        in_specs=[VMEM, VMEM, VMEM, ANY],
        out_specs=VMEM,
        scratch_shapes=scratch,
        compiler_params=params(16),
        cost_estimate=cost(40 * noise.size, 4 * noise.size),
        name="local1",
    )(coef, halo, tiled1, own[0])
    near = pl.pallas_call(
        edges,
        out_shape=jax.ShapeDtypeStruct((GROUP, 2, 8, TILE), F32),
        in_specs=[VMEM] * GROUP + [ANY],
        out_specs=VMEM,
        compiler_params=params(4),
        name="edges",
    )(*states, local1)
    near = xor_permute(near, "gx", 1)
    out = [
        jax.ShapeDtypeStruct(noise.shape, F32),
        jax.ShapeDtypeStruct((levels, ys, columns), F32),
    ]
    latent, soft = pl.pallas_call(
        finish,
        out_shape=out,
        in_specs=[VMEM] * 9,
        out_specs=[ANY, ANY],
        scratch_shapes=[
            pltpu.VMEM((2, 2, ys, columns + TILE), F32),
            pltpu.VMEM(noise.shape, F32),
            pltpu.VMEM((levels, ys, columns), F32),
            pltpu.SemaphoreType.DMA((8, 2)),
        ],
        compiler_params=params(24),
        name="finish",
    )(local0, local1, reach, bias, *states, near)
    return latent, soft


def solution(mesh):
    return jax.shard_map(
        shards,
        mesh=mesh,
        in_specs=(
            P(("parts", "gz"), None, None, "gx"),
            P(("parts", "gz"), None),
            P(),
            P("parts", "gx"),
            P(),
        ),
        out_specs=(P(("parts", "gz"), None, None, "gx"), P(("parts", "gz"), None, "gx")),
        check_vma=False,
    )
```

```python
import functools

import jax
import jax.numpy as jnp
from jax import lax
from jax.experimental import pallas as pl
from jax.experimental.pallas import tpu as pltpu
from jax.sharding import PartitionSpec as P

SWEEPS = 4
GROUP = 4
TILE = 128
F32 = jnp.float32
SMEM = pl.BlockSpec(memory_space=pltpu.SMEM)
ANY = pl.BlockSpec(memory_space=pl.ANY)
VMEM = pl.BlockSpec(memory_space=pltpu.VMEM)
HBM = pl.BlockSpec(memory_space=pltpu.HBM)


def splat(value):
    return jnp.full((8, TILE), value, F32)


def row(ref, *at):
    return jnp.broadcast_to(ref[(*at[:-1], pl.ds(at[-1], 1), slice(None))], (8, TILE))


def coefficients(scale_index, rates):
    slots = jnp.arange(rates.shape[0], dtype=jnp.int32)
    hits = (scale_index.T[..., None] == slots).astype(F32)
    alpha = jnp.exp(-jnp.sum(hits * rates, axis=-1))
    both = jnp.stack([alpha, jnp.sqrt(1.0 - alpha * alpha)])
    return jnp.broadcast_to(both[..., None], (*both.shape, TILE))


def position():
    return lax.rem(lax.axis_index("gz"), GROUP)


def carries(coef, noise_hbm, out0, out1, out2, out3, packed, tiled0, tiled1, held, pre, wts, sems):
    outs, tiled = (out0, out1, out2, out3), (tiled0, tiled1)
    levels, columns = noise_hbm.shape[0], noise_hbm.shape[3]
    tiles = columns // TILE
    pos = position()
    core = lax.axis_index("gx")
    copies = []
    for s in range(GROUP):
        rows = slice(8 * (s % 2), 8 * (s % 2) + 8)
        copies.append([])
        for t in range(tiles):
            source = noise_hbm.at[:, s // 2, rows, pl.ds(t * TILE, TILE)]
            copies[s].append(pltpu.make_async_copy(source, tiled[s // 2].at[t, :, rows, :], sems.at[s, t]))
            copies[s][t].start()
    for field in range(2):
        run = splat(1.0)
        for k in range(levels):
            pre[k] = run
            run = run * row(coef, 0, field, k)
        total = run
        post, gather, after = splat(1.0), splat(0.0), splat(0.0)
        for k in reversed(range(levels)):
            alpha, gain = row(coef, 0, field, k), row(coef, 1, field, k)
            gather = pre[k] * (1.0 - alpha) + after * gather
            wts[0, field, k] = gain * post
            wts[1, field, k] = gain * gather
            post = post * alpha
            after = alpha
        wts[0, field, levels] = total
        wts[1, field, levels] = after * gather
    near = (1 - core) * (tiles - 1)
    for s in range(GROUP):
        for copy in copies[s]:
            copy.wait()
        field, k = s // 2, pos ^ s
        rows = slice(8 * (s % 2), 8 * (s % 2) + 8)
        for half in range(2):
            ours = range(half * tiles // 2, (half + 1) * tiles // 2)

            def body(level, sums, field=field, rows=rows, ours=ours):
                fwd, bwd = wts[0, field, level], wts[1, field, level]
                new = []
                for t, (one, two) in zip(ours, sums):
                    value = tiled[field][t, level, rows, :]
                    new.append((one + fwd * value, two + bwd * value))
                return tuple(new)

            sums = lax.fori_loop(0, levels, body, ((splat(0.0), splat(0.0)),) * len(ours), unroll=True)
            for t, (one, two) in zip(ours, sums):
                held[k, 0, :, t * TILE : (t + 1) * TILE] = one
                held[k, 1, :, t * TILE : (t + 1) * TILE] = two
        held[k, 0, :, columns:] = wts[0, field, levels]
        held[k, 1, :, columns:] = wts[1, field, levels]
    for k in range(GROUP):
        outs[k][...] = held[k]
    for field in range(2):
        flat = tiled[field].reshape(tiles, levels * 16, TILE)
        for first in range(0, 16, TILE // levels):
            rows = [
                flat[near, pl.ds(8 * g * 16 + y, 8, stride=16), :]
                for y in range(first, first + TILE // levels)
                for g in range(levels // 8)
            ]
            turned = jnp.concatenate(rows, axis=0).T
            packed[field, first * levels // TILE] = jnp.where(core == 0, turned[TILE - 8 :], turned[:8])


def scan_group(held, lanes, f_in, r_in):
    columns = held.shape[3] - TILE
    f = [f_in]
    for j in range(GROUP):
        f.append(held[j, 0, :, columns:] * f[j] + held[j, 0, :, lanes])
    r = [None] * GROUP + [r_in]
    for j in reversed(range(GROUP)):
        r[j] = held[j, 1, :, lanes] + held[j, 1, :, columns:] * f[j] + held[j, 0, :, columns:] * r[j + 1]
    return f, r


def hold(refs, held):
    pos = position()
    for k, ref in enumerate(refs):
        held[pos ^ k] = ref[...]


def group_total(m0, m1, m2, m3, after, out, held):
    hold((m0, m1, m2, m3), held)
    columns = held.shape[3] - TILE
    zero = splat(0.0)
    for t in range(columns // TILE):
        lanes = slice(t * TILE, (t + 1) * TILE)
        f, r = scan_group(held, lanes, zero, zero)
        out[0, :, lanes] = f[GROUP]
        out[1, :, lanes] = r[0]
    run, factor = splat(1.0), splat(0.0)
    for j in range(GROUP):
        run = run * held[j, 0, :, columns:]
    for j in reversed(range(GROUP)):
        a, c = held[j, 0, :, columns:], held[j, 1, :, columns:]
        factor = c + a * a * factor
    out[0, :, columns:] = run
    out[1, :, columns:] = factor


def enter_group(m0, m1, m2, m3, entering, after, out0, out1, out2, out3, held):
    hold((m0, m1, m2, m3), held)
    columns = held.shape[3] - TILE
    outs = (out0, out1, out2, out3)
    pos = position()
    for t in range(columns // TILE):
        lanes = slice(t * TILE, (t + 1) * TILE)
        f, r = scan_group(held, lanes, entering[0, :, lanes], entering[1, :, lanes])
        for j in range(GROUP):
            held[j, 0, :, lanes] = f[j]
            held[j, 1, :, lanes] = r[j + 1]
    for k in range(GROUP):
        outs[k][...] = held[pos ^ k, :, :, :columns]


def diffuse(work, tiles, keep):
    fields = work.shape[1]
    lane = lax.broadcasted_iota(jnp.int32, (8, TILE), 1)
    line = lax.broadcasted_iota(jnp.int32, (8, TILE), 0)
    for turn in range(SWEEPS):
        src, dst = turn % 2, 1 - turn % 2
        for field in range(fields):
            for t in range(tiles):
                pair = [work[src, field, half, t] for half in range(2)]
                above = [pltpu.roll(v, 1, 0) for v in pair]
                below = [pltpu.roll(v, 7, 0) for v in pair]
                above = [jnp.where(line == 0, 0.0, above[0]), jnp.where(line == 0, above[0], above[1])]
                below = [jnp.where(line == 7, below[1], below[0]), jnp.where(line == 7, 0.0, below[1])]
                for half, value in enumerate(pair):
                    before = work[src, field, half, (t - 1) % tiles]
                    later = work[src, field, half, (t + 1) % tiles]
                    side = pltpu.roll(jnp.where(lane == TILE - 1, before, value), 1, 1)
                    side += pltpu.roll(jnp.where(lane == 0, later, value), TILE - 1, 1)
                    new = value + side + (above[half] + below[half])
                    work[dst, field, half, t] = new * keep if t == tiles - 1 else new


def edge_mask():
    lane = lax.broadcasted_iota(jnp.int32, (8, TILE), 1)
    core = lax.axis_index("gx")
    return ((lane < TILE // 2) == (core == 0)).astype(F32)


def prepare(coef, codes, thresholds, after, reach, bias, pre):
    levels = coef.shape[2]
    for field in range(2):
        run = splat(1.0)
        for k in range(levels):
            run = run * row(coef, 0, field, k)
            pre[k] = run
        down, up = splat(0.0), splat(1.0)
        for k in reversed(range(levels)):
            alpha = row(coef, 0, field, k)
            down = alpha * down + (1.0 - alpha) * pre[k]
            up = alpha * up
            reach[0, field, k : k + 1, :] = down[:1]
            reach[1, field, k : k + 1, :] = up[:1]
    code = codes[...]
    value = jnp.zeros(code.shape, F32)
    for i in range(thresholds.shape[0]):
        value = jnp.where(code == i, thresholds[i], value)
    bias[...] = value


def local_first(coef, packed, tiled, noise_hbm, out, tiled_next, buf, work, sems):
    copies = [
        pltpu.make_async_copy(noise_hbm.at[:, 1, :, pl.ds(t * TILE, TILE)], tiled_next.at[t], sems.at[t])
        for t in range(tiled.shape[0])
    ]
    for copy in copies:
        copy.start()
    local_field(0, coef, packed, tiled, None, out, buf, work)
    for copy in copies:
        copy.wait()


def local_field(field, coef, packed, tiled, after, out, buf, work):
    tiles, levels, ys, _ = tiled.shape
    columns = tiles * TILE
    ranges = TILE // levels
    span = columns // ranges
    blocks = span // TILE
    main = 16
    core = lax.axis_index("gx")
    lane = lax.broadcasted_iota(jnp.int32, (8, TILE), 1)
    keep_left = (lane >= levels) | (core == 1)
    keep_right = (lane < TILE - levels) | (core == 0)
    source = tiled.reshape(tiles, levels * ys, TILE)
    flat = buf.reshape(tiles, levels * ys, TILE)
    for slot in range(2):
        for y in range(ys):
            work[slot, y, 0:8, :] = splat(0.0)
            work[slot, y, main + span + 8 :, :] = splat(0.0)

    def pieces(y):
        return [(c, g, pl.ds(8 * g * ys + y, 8, stride=ys)) for c in range(ranges) for g in range(levels // 8)]

    for y in range(ys):
        for b in range(blocks):
            rows = [source[c * blocks + b, at, :] for c, g, at in pieces(y)]
            work[0, y, main + b * TILE : main + (b + 1) * TILE, :] = jnp.concatenate(rows, axis=0).T
        edge, place = packed[field, y // ranges], y % ranges
        left = pltpu.roll(work[0, y, main + span - 8 : main + span, :], levels, 1)
        right = pltpu.roll(work[0, y, main : main + 8, :], TILE - levels, 1)
        far_left = pltpu.roll(edge, (TILE - levels * place) % TILE, 1)
        far_right = pltpu.roll(edge, levels * (ranges - 1 - place), 1)
        left = jnp.where(keep_left, jnp.where(lane < levels, far_left, left), 0.0)
        right = jnp.where(keep_right, jnp.where(lane >= TILE - levels, far_right, right), 0.0)
        work[0, y, main - 8 : main, :] = left
        work[0, y, main + span : main + span + 8, :] = right

    def block(src, at, before, later, keep=None):
        above, here = splat(0.0), work[src, 0, at, :]
        for y in range(ys):
            below = work[src, y + 1, at, :] if y + 1 < ys else splat(0.0)
            new = here + (work[src, y, before, :] + work[src, y, later, :]) + (above + below)
            if keep is not None:
                new = jnp.where(keep, new, 0.0)
            work[1 - src, y, at, :] = new
            above, here = here, below

    for turn in range(SWEEPS):
        src = turn % 2

        def step(r, _, src=src):
            at = pl.multiple_of(main + 8 * r, 8)
            block(src, pl.ds(at, 8), pl.ds(at - 1, 8), pl.ds(at + 1, 8))
            return 0

        lax.fori_loop(0, span // 8, step, 0, unroll=True)
        if turn + 1 < SWEEPS:
            for at, keep in ((main - 8, keep_left), (main + span, keep_right)):
                block(src, pl.ds(at, 8), pl.ds(at - 1, 8), pl.ds(at + 1, 8), keep)
    for y in range(ys):
        for b in range(blocks):
            turned = work[SWEEPS % 2, y, main + b * TILE : main + (b + 1) * TILE, :].T
            for i, (c, g, at) in enumerate(pieces(y)):
                flat[c * blocks + b, at, :] = turned[8 * i : 8 * i + 8]
    scale = 0.2**SWEEPS
    spots = [(t, top) for t in range(tiles) for top in range(ys // 8)]

    def forward(level, state):
        alpha, gain = row(coef, 0, field, level), row(coef, 1, field, level) * scale
        new = []
        for (t, top), old in zip(spots, state):
            value = alpha * old + gain * buf[t, level, 8 * top : 8 * top + 8, :]
            buf[t, level, 8 * top : 8 * top + 8, :] = value
            new.append(value)
        return tuple(new)

    def backward(turn, state):
        level = levels - 1 - turn
        alpha = row(coef, 0, field, level)
        gain = 1.0 - alpha
        new = []
        for (t, top), old in zip(spots, state):
            value = alpha * old + gain * buf[t, level, 8 * top : 8 * top + 8, :]
            out[level, 8 * top : 8 * top + 8, t * TILE : (t + 1) * TILE] = value
            new.append(value)
        return tuple(new)

    zeros = (splat(0.0),) * len(spots)
    lax.fori_loop(0, levels, forward, zeros, unroll=True)
    lax.fori_loop(0, levels, backward, zeros, unroll=True)


def edges(m0, m1, m2, m3, after, out):
    columns = m0.shape[2]
    near = pl.ds(pl.multiple_of((1 - lax.axis_index("gx")) * (columns - TILE), TILE), TILE)
    for k, ref in enumerate((m0, m1, m2, m3)):
        out[k] = ref[:, :, near]


def spread(m0, m1, m2, m3, after, out, work):
    columns = m0.shape[2]
    tiles = columns // TILE
    pos = position()
    for k, ref in enumerate((m0, m1, m2, m3)):
        s = pos ^ k
        for kind in range(2):
            for t in range(tiles):
                work[0, 2 * kind + s // 2, s % 2, t] = ref[kind, :, t * TILE : (t + 1) * TILE]
    for field in range(4):
        for half in range(2):
            work[0, field, half, tiles] = splat(0.0)
    diffuse(work, tiles + 1, edge_mask())
    for field in range(4):
        for half in range(2):
            for t in range(tiles):
                at = (field // 2, field % 2, slice(8 * half, 8 * half + 8), slice(t * TILE, (t + 1) * TILE))
                out[at] = work[SWEEPS % 2, field, half, t] * 0.2**SWEEPS


def finish(g0, g1, reach, bias, own, halo, latent_hbm, soft_hbm, state, work, latent, soft, sems):
    levels, columns = g0.shape[0], g0.shape[2]
    pos = position()
    keep = edge_mask()
    for k in range(GROUP):
        s = pos ^ k
        for kind in range(2):
            work[0, 2 * kind + s // 2, s % 2, 1] = halo[k, kind] * keep
            work[0, 2 * kind + s // 2, s % 2, 0] = splat(0.0)
    diffuse(work, 2, keep)
    state[...] = own[...]
    near = pl.ds(pl.multiple_of((1 - lax.axis_index("gx")) * (columns - TILE), TILE), TILE)
    for field in range(4):
        for half in range(2):
            at = (field // 2, field % 2, slice(8 * half, 8 * half + 8), near)
            state[at] += work[SWEEPS % 2, field, half, 0] * 0.2**SWEEPS
    parts = sems.shape[0]
    step = levels // parts
    tiles = columns // TILE
    copies = []
    for i in range(parts):

        def body(turn, _, i=i):
            rows = pl.ds(pl.multiple_of(8 * (turn // tiles), 8), 8)
            lanes = pl.ds(pl.multiple_of(TILE * lax.rem(turn, tiles), TILE), TILE)
            f = [state[0, field, rows, lanes] for field in range(2)]
            r = [state[1, field, rows, lanes] for field in range(2)]
            base = bias[rows, lanes]
            for level in range(i * step, (i + 1) * step):
                one = g0[level, rows, lanes] + row(reach, 0, 0, level) * f[0] + row(reach, 1, 0, level) * r[0]
                two = g1[level, rows, lanes] + row(reach, 0, 1, level) * f[1] + row(reach, 1, 1, level) * r[1]
                latent[level, 0, rows, lanes] = one
                latent[level, 1, rows, lanes] = two
                half = 0.5 + 0.5 * jnp.tanh(1.5 * (one - base))
                soft[level, rows, lanes] = half * (0.5 + 0.5 * jnp.tanh(1.5 * two))
            return 0

        lax.fori_loop(0, 2 * tiles, body, 0, unroll=True)
        at = pl.ds(i * step, step)
        copies += [
            pltpu.make_async_copy(latent.at[at], latent_hbm.at[at], sems.at[i, 0]),
            pltpu.make_async_copy(soft.at[at], soft_hbm.at[at], sems.at[i, 1]),
        ]
        for copy in copies[-2:]:
            copy.start()
    for copy in copies:
        copy.wait()


def params(mib):
    return pltpu.CompilerParams(vmem_limit_bytes=mib << 20)


def cost(flops, data):
    return pl.CostEstimate(flops=flops, bytes_accessed=data, transcendentals=0)


def xor_permute(value, axis, by):
    return lax.ppermute(value, axis, [(i, i ^ by) for i in range(lax.axis_size(axis))])


def entering_states(total, groups):
    columns = total.shape[2] - TILE
    group = lax.axis_index("gz") // GROUP

    def wide(value):
        return jnp.tile(value, (1, columns // TILE))

    def fwd(t):
        return t[0, :, :columns]

    def bwd(t):
        return t[1, :, :columns]

    if groups == 2:
        sent = jnp.where(group == 0, jnp.concatenate([total[0, :, :columns], total[0, :, columns:]], axis=1),
                         total[1])
        got = xor_permute(sent, "gz", GROUP)
        zero = jnp.zeros((8, columns), F32)
        below = got[:, :columns] + wide(got[:, columns:]) * fwd(total)
        return jnp.stack([jnp.where(group == 0, zero, got[:, :columns]), jnp.where(group == 0, below, zero)])
    size = GROUP * groups
    totals = [total]
    for turn in range(1, groups):
        totals.append(lax.ppermute(total, "gz", [(i, (i + GROUP * turn) % size) for i in range(size)]))
    stacked = jnp.stack(totals)
    state = jnp.zeros((8, columns), F32)
    f = [state]
    at = [lax.dynamic_index_in_dim(stacked, (group - j) % groups, keepdims=False) for j in range(groups)]
    for j in range(groups):
        state = wide(at[j][0, :, columns:]) * state + fwd(at[j])
        f.append(state)
    state = jnp.zeros((8, columns), F32)
    r = [None] * groups + [state]
    for j in reversed(range(groups)):
        state = bwd(at[j]) + wide(at[j][1, :, columns:]) * f[j] + wide(at[j][0, :, columns:]) * state
        r[j] = state
    return jnp.stack(
        [
            lax.dynamic_index_in_dim(jnp.stack(f[:groups]), group, keepdims=False),
            lax.dynamic_index_in_dim(jnp.stack(r[1:]), group, keepdims=False),
        ]
    )


def shards(noise, scale_index, rates, facies_code, thresholds):
    levels, _, ys, columns = noise.shape
    assert ys == 16 and levels % 8 == 0 and TILE % levels == 0 and columns * levels % (TILE * TILE) == 0
    tiles = columns // TILE
    groups = lax.axis_size("gz") // GROUP
    message = jax.ShapeDtypeStruct((2, 8, columns + TILE), F32)
    coef = coefficients(scale_index, rates)
    *mine, packed, tiled0 = pl.pallas_call(
        carries,
        out_shape=[message] * GROUP
        + [
            jax.ShapeDtypeStruct((2, ys * levels // TILE, 8, TILE), F32),
            jax.ShapeDtypeStruct((tiles, levels, ys, TILE), F32),
        ],
        in_specs=[VMEM, HBM],
        out_specs=[VMEM] * (GROUP + 2),
        scratch_shapes=[
            pltpu.VMEM((tiles, levels, ys, TILE), F32),
            pltpu.VMEM((GROUP, 2, 8, columns + TILE), F32),
            pltpu.VMEM((levels, 8, TILE), F32),
            pltpu.VMEM((2, 2, levels + 1, 8, TILE), F32),
            pltpu.SemaphoreType.DMA((GROUP, tiles)),
        ],
        compiler_params=params(50),
        cost_estimate=cost(4 * noise.size, 4 * noise.size),
        name="carries",
    )(coef, noise)
    got = [mine[0]] + [xor_permute(mine[k], "gz", k) for k in range(1, GROUP)]
    halo = xor_permute(packed, "gx", 1)

    field_out = jax.ShapeDtypeStruct((levels, ys, columns), F32)
    field_tiled = jax.ShapeDtypeStruct((tiles, levels, ys, TILE), F32)
    scratch = [
        pltpu.VMEM((tiles, levels, ys, TILE), F32),
        pltpu.VMEM((2, ys, columns * levels // TILE + 32, TILE), F32),
    ]
    local0, tiled1 = pl.pallas_call(
        local_first,
        out_shape=[field_out, field_tiled],
        in_specs=[VMEM, VMEM, VMEM, HBM],
        out_specs=[VMEM] * 2,
        scratch_shapes=[*scratch, pltpu.SemaphoreType.DMA((tiles,))],
        compiler_params=params(45),
        cost_estimate=cost(40 * noise.size, 4 * noise.size),
        name="local0",
    )(coef, halo, tiled0, noise)
    held = pltpu.VMEM((GROUP, 2, 8, columns + TILE), F32)
    total = pl.pallas_call(
        group_total,
        out_shape=message,
        in_specs=[VMEM] * GROUP + [ANY],
        out_specs=VMEM,
        scratch_shapes=[held],
        compiler_params=params(8),
        name="group_total",
    )(*got, local0)
    reach, bias = pl.pallas_call(
        prepare,
        out_shape=[
            jax.ShapeDtypeStruct((2, 2, levels, TILE), F32),
            jax.ShapeDtypeStruct((ys, columns), F32),
        ],
        in_specs=[VMEM, VMEM, SMEM, ANY],
        out_specs=[VMEM] * 2,
        scratch_shapes=[pltpu.VMEM((levels, 8, TILE), F32)],
        compiler_params=params(4),
        cost_estimate=cost(noise.size, noise.size),
        name="prepare",
    )(coef, facies_code, thresholds, total)
    entering = entering_states(total, groups)
    state = jax.ShapeDtypeStruct((2, 8, columns), F32)
    own = pl.pallas_call(
        enter_group,
        out_shape=[state] * GROUP,
        in_specs=[VMEM] * (GROUP + 1) + [ANY],
        out_specs=[VMEM] * GROUP,
        scratch_shapes=[held],
        compiler_params=params(8),
        name="enter_group",
    )(*got, entering, reach)
    states = [own[0]] + [xor_permute(own[k], "gz", k) for k in range(1, GROUP)]
    local1 = pl.pallas_call(
        functools.partial(local_field, 1),
        out_shape=field_out,
        in_specs=[VMEM, VMEM, VMEM, ANY],
        out_specs=VMEM,
        scratch_shapes=scratch,
        compiler_params=params(16),
        cost_estimate=cost(40 * noise.size, 4 * noise.size),
        name="local1",
    )(coef, halo, tiled1, own[0])
    near = pl.pallas_call(
        edges,
        out_shape=jax.ShapeDtypeStruct((GROUP, 2, 8, TILE), F32),
        in_specs=[VMEM] * GROUP + [ANY],
        out_specs=VMEM,
        compiler_params=params(4),
        name="edges",
    )(*states, local1)
    spread_out = pl.pallas_call(
        spread,
        out_shape=jax.ShapeDtypeStruct((2, 2, ys, columns), F32),
        in_specs=[VMEM] * GROUP + [ANY],
        out_specs=VMEM,
        scratch_shapes=[pltpu.VMEM((2, 4, 2, tiles + 1, 8, TILE), F32)],
        compiler_params=params(8),
        cost_estimate=cost(4 * noise.size, noise.size),
        name="spread",
    )(*states, near)
    near = xor_permute(near, "gx", 1)
    out = [
        jax.ShapeDtypeStruct(noise.shape, F32),
        jax.ShapeDtypeStruct((levels, ys, columns), F32),
    ]
    latent, soft = pl.pallas_call(
        finish,
        out_shape=out,
        in_specs=[VMEM] * 6,
        out_specs=[ANY, ANY],
        scratch_shapes=[
            pltpu.VMEM((2, 2, ys, columns), F32),
            pltpu.VMEM((2, 4, 2, 2, 8, TILE), F32),
            pltpu.VMEM(noise.shape, F32),
            pltpu.VMEM((levels, ys, columns), F32),
            pltpu.SemaphoreType.DMA((8, 2)),
        ],
        compiler_params=params(24),
        name="finish",
    )(local0, local1, reach, bias, spread_out, near)
    return latent, soft


def solution(mesh):
    return jax.shard_map(
        shards,
        mesh=mesh,
        in_specs=(
            P(("parts", "gz"), None, None, "gx"),
            P(("parts", "gz"), None),
            P(),
            P("parts", "gx"),
            P(),
        ),
        out_specs=(P(("parts", "gz"), None, None, "gx"), P(("parts", "gz"), None, "gx")),
        check_vma=False,
    )
```

```python
import functools

import jax
import jax.numpy as jnp
from jax import lax
from jax.experimental import pallas as pl
from jax.experimental.pallas import tpu as pltpu
from jax.sharding import PartitionSpec as P

SWEEPS = 4
GROUP = 4
TILE = 128
F32 = jnp.float32
SMEM = pl.BlockSpec(memory_space=pltpu.SMEM)
ANY = pl.BlockSpec(memory_space=pl.ANY)
VMEM = pl.BlockSpec(memory_space=pltpu.VMEM)
HBM = pl.BlockSpec(memory_space=pltpu.HBM)


def splat(value):
    return jnp.full((8, TILE), value, F32)


def row(ref, *at):
    return jnp.broadcast_to(ref[(*at[:-1], pl.ds(at[-1], 1), slice(None))], (8, TILE))


def fill_tables(rates, table):
    for i in range(rates.shape[0]):
        alpha = jnp.exp(-splat(rates[i]))
        table[0, i] = alpha
        table[1, i] = jnp.sqrt(1.0 - alpha * alpha)


def position():
    return lax.rem(lax.axis_index("gz"), GROUP)


def carries(idx_hbm, rates_hbm, noise_hbm, out0, out1, out2, out3, coef, packed, tiled0, tiled1, held, table, pre, wts, idx, rates, sems):
    outs, tiled = (out0, out1, out2, out3), (tiled0, tiled1)
    levels, columns = noise_hbm.shape[0], noise_hbm.shape[3]
    tiles = columns // TILE
    pos = position()
    core = lax.axis_index("gx")
    small = [
        pltpu.make_async_copy(idx_hbm, idx, sems.at[GROUP, 0]),
        pltpu.make_async_copy(rates_hbm, rates, sems.at[GROUP, 1]),
    ]
    for copy in small:
        copy.start()
    copies = []
    for s in range(GROUP):
        rows = slice(8 * (s % 2), 8 * (s % 2) + 8)
        copies.append([])
        for t in range(tiles):
            source = noise_hbm.at[:, s // 2, rows, pl.ds(t * TILE, TILE)]
            copies[s].append(pltpu.make_async_copy(source, tiled[s // 2].at[t, :, rows, :], sems.at[s, t]))
            copies[s][t].start()
    for copy in small:
        copy.wait()
    fill_tables(rates, table)
    for field in range(2):
        run = splat(1.0)
        for k in range(levels):
            pre[k] = run
            run = run * table[0, idx[field, k]]
        total = run
        post, gather, after = splat(1.0), splat(0.0), splat(0.0)
        for k in reversed(range(levels)):
            alpha, gain = table[0, idx[field, k]], table[1, idx[field, k]]
            coef[0, field, k : k + 1, :] = alpha[:1]
            coef[1, field, k : k + 1, :] = gain[:1]
            gather = pre[k] * (1.0 - alpha) + after * gather
            wts[0, field, k] = gain * post
            wts[1, field, k] = gain * gather
            post = post * alpha
            after = alpha
        wts[0, field, levels] = total
        wts[1, field, levels] = after * gather
    near = (1 - core) * (tiles - 1)
    for s in range(GROUP):
        for copy in copies[s]:
            copy.wait()
        field, k = s // 2, pos ^ s
        rows = slice(8 * (s % 2), 8 * (s % 2) + 8)
        for half in range(2):
            ours = range(half * tiles // 2, (half + 1) * tiles // 2)

            def body(level, sums, field=field, rows=rows, ours=ours):
                fwd, bwd = wts[0, field, level], wts[1, field, level]
                new = []
                for t, (one, two) in zip(ours, sums):
                    value = tiled[field][t, level, rows, :]
                    new.append((one + fwd * value, two + bwd * value))
                return tuple(new)

            sums = lax.fori_loop(0, levels, body, ((splat(0.0), splat(0.0)),) * len(ours), unroll=True)
            for t, (one, two) in zip(ours, sums):
                held[k, 0, :, t * TILE : (t + 1) * TILE] = one
                held[k, 1, :, t * TILE : (t + 1) * TILE] = two
        held[k, 0, :, columns:] = wts[0, field, levels]
        held[k, 1, :, columns:] = wts[1, field, levels]
        if s % 2 == 0:
            continue
        flat = tiled[field].reshape(tiles, levels * 16, TILE)
        for first in range(0, 16, TILE // levels):
            parts = [
                flat[near, pl.ds(8 * g * 16 + y, 8, stride=16), :]
                for y in range(first, first + TILE // levels)
                for g in range(levels // 8)
            ]
            turned = jnp.concatenate(parts, axis=0).T
            packed[field, first * levels // TILE] = jnp.where(core == 0, turned[TILE - 8 :], turned[:8])
    for k in range(GROUP):
        outs[k][...] = held[k]


def scan_group(held, lanes, f_in, r_in):
    columns = held.shape[3] - TILE
    f = [f_in]
    for j in range(GROUP):
        f.append(held[j, 0, :, columns:] * f[j] + held[j, 0, :, lanes])
    r = [None] * GROUP + [r_in]
    for j in reversed(range(GROUP)):
        r[j] = held[j, 1, :, lanes] + held[j, 1, :, columns:] * f[j] + held[j, 0, :, columns:] * r[j + 1]
    return f, r


def hold(refs, held):
    pos = position()
    for k, ref in enumerate(refs):
        held[pos ^ k] = ref[...]


def group_total(m0, m1, m2, m3, after, out, held):
    hold((m0, m1, m2, m3), held)
    columns = held.shape[3] - TILE
    zero = splat(0.0)
    for t in range(columns // TILE):
        lanes = slice(t * TILE, (t + 1) * TILE)
        f, r = scan_group(held, lanes, zero, zero)
        out[0, :, lanes] = f[GROUP]
        out[1, :, lanes] = r[0]
    run, factor = splat(1.0), splat(0.0)
    for j in range(GROUP):
        run = run * held[j, 0, :, columns:]
    for j in reversed(range(GROUP)):
        a, c = held[j, 0, :, columns:], held[j, 1, :, columns:]
        factor = c + a * a * factor
    out[0, :, columns:] = run
    out[1, :, columns:] = factor


def enter_group(m0, m1, m2, m3, entering, after, out0, out1, out2, out3, held):
    hold((m0, m1, m2, m3), held)
    columns = held.shape[3] - TILE
    outs = (out0, out1, out2, out3)
    pos = position()
    for t in range(columns // TILE):
        lanes = slice(t * TILE, (t + 1) * TILE)
        f, r = scan_group(held, lanes, entering[0, :, lanes], entering[1, :, lanes])
        for j in range(GROUP):
            held[j, 0, :, lanes] = f[j]
            held[j, 1, :, lanes] = r[j + 1]
    for k in range(GROUP):
        outs[k][...] = held[pos ^ k, :, :, :columns]


def diffuse(work, tiles, keep):
    fields = work.shape[1]
    lane = lax.broadcasted_iota(jnp.int32, (8, TILE), 1)
    line = lax.broadcasted_iota(jnp.int32, (8, TILE), 0)
    for turn in range(SWEEPS):
        src, dst = turn % 2, 1 - turn % 2
        for field in range(fields):
            for t in range(tiles):
                pair = [work[src, field, half, t] for half in range(2)]
                above = [pltpu.roll(v, 1, 0) for v in pair]
                below = [pltpu.roll(v, 7, 0) for v in pair]
                above = [jnp.where(line == 0, 0.0, above[0]), jnp.where(line == 0, above[0], above[1])]
                below = [jnp.where(line == 7, below[1], below[0]), jnp.where(line == 7, 0.0, below[1])]
                for half, value in enumerate(pair):
                    before = work[src, field, half, (t - 1) % tiles]
                    later = work[src, field, half, (t + 1) % tiles]
                    side = pltpu.roll(jnp.where(lane == TILE - 1, before, value), 1, 1)
                    side += pltpu.roll(jnp.where(lane == 0, later, value), TILE - 1, 1)
                    new = value + side + (above[half] + below[half])
                    work[dst, field, half, t] = new * keep if t == tiles - 1 else new


def edge_mask():
    lane = lax.broadcasted_iota(jnp.int32, (8, TILE), 1)
    core = lax.axis_index("gx")
    return ((lane < TILE // 2) == (core == 0)).astype(F32)


def prepare(coef, codes, thresholds, after, reach, bias, pre):
    levels = coef.shape[2]
    for field in range(2):
        run = splat(1.0)
        for k in range(levels):
            run = run * row(coef, 0, field, k)
            pre[k] = run
        down, up = splat(0.0), splat(1.0)
        for k in reversed(range(levels)):
            alpha = row(coef, 0, field, k)
            down = alpha * down + (1.0 - alpha) * pre[k]
            up = alpha * up
            reach[0, field, k : k + 1, :] = down[:1]
            reach[1, field, k : k + 1, :] = up[:1]
    code = codes[...]
    value = jnp.zeros(code.shape, F32)
    for i in range(thresholds.shape[0]):
        value = jnp.where(code == i, thresholds[i], value)
    bias[...] = value


def local_first(coef, packed, tiled, noise_hbm, out, tiled_next, buf, work, sems):
    copies = [
        pltpu.make_async_copy(noise_hbm.at[:, 1, :, pl.ds(t * TILE, TILE)], tiled_next.at[t], sems.at[t])
        for t in range(tiled.shape[0])
    ]
    for copy in copies:
        copy.start()
    local_field(0, coef, packed, tiled, None, out, buf, work)
    for copy in copies:
        copy.wait()


def local_field(field, coef, packed, tiled, after, out, buf, work):
    tiles, levels, ys, _ = tiled.shape
    columns = tiles * TILE
    ranges = TILE // levels
    span = columns // ranges
    blocks = span // TILE
    main = 16
    core = lax.axis_index("gx")
    lane = lax.broadcasted_iota(jnp.int32, (8, TILE), 1)
    keep_left = (lane >= levels) | (core == 1)
    keep_right = (lane < TILE - levels) | (core == 0)
    source = tiled.reshape(tiles, levels * ys, TILE)
    flat = buf.reshape(tiles, levels * ys, TILE)
    for slot in range(2):
        for y in range(ys):
            work[slot, y, 0:8, :] = splat(0.0)
            work[slot, y, main + span + 8 :, :] = splat(0.0)

    def pieces(y):
        return [(c, g, pl.ds(8 * g * ys + y, 8, stride=ys)) for c in range(ranges) for g in range(levels // 8)]

    for y in range(ys):
        for b in range(blocks):
            rows = [source[c * blocks + b, at, :] for c, g, at in pieces(y)]
            work[0, y, main + b * TILE : main + (b + 1) * TILE, :] = jnp.concatenate(rows, axis=0).T
        edge, place = packed[field, y // ranges], y % ranges
        left = pltpu.roll(work[0, y, main + span - 8 : main + span, :], levels, 1)
        right = pltpu.roll(work[0, y, main : main + 8, :], TILE - levels, 1)
        far_left = pltpu.roll(edge, (TILE - levels * place) % TILE, 1)
        far_right = pltpu.roll(edge, levels * (ranges - 1 - place), 1)
        left = jnp.where(keep_left, jnp.where(lane < levels, far_left, left), 0.0)
        right = jnp.where(keep_right, jnp.where(lane >= TILE - levels, far_right, right), 0.0)
        work[0, y, main - 8 : main, :] = left
        work[0, y, main + span : main + span + 8, :] = right

    def block(src, at, before, later, keep=None):
        above, here = splat(0.0), work[src, 0, at, :]
        for y in range(ys):
            below = work[src, y + 1, at, :] if y + 1 < ys else splat(0.0)
            new = here + (work[src, y, before, :] + work[src, y, later, :]) + (above + below)
            if keep is not None:
                new = jnp.where(keep, new, 0.0)
            work[1 - src, y, at, :] = new
            above, here = here, below

    for turn in range(SWEEPS):
        src = turn % 2

        def step(r, _, src=src):
            at = pl.multiple_of(main + 8 * r, 8)
            block(src, pl.ds(at, 8), pl.ds(at - 1, 8), pl.ds(at + 1, 8))
            return 0

        lax.fori_loop(0, span // 8, step, 0, unroll=True)
        if turn + 1 < SWEEPS:
            for at, keep in ((main - 8, keep_left), (main + span, keep_right)):
                block(src, pl.ds(at, 8), pl.ds(at - 1, 8), pl.ds(at + 1, 8), keep)
    for y in range(ys):
        for b in range(blocks):
            turned = work[SWEEPS % 2, y, main + b * TILE : main + (b + 1) * TILE, :].T
            for i, (c, g, at) in enumerate(pieces(y)):
                flat[c * blocks + b, at, :] = turned[8 * i : 8 * i + 8]
    scale = 0.2**SWEEPS
    spots = [(t, top) for t in range(tiles) for top in range(ys // 8)]

    def forward(level, state):
        alpha, gain = row(coef, 0, field, level), row(coef, 1, field, level) * scale
        new = []
        for (t, top), old in zip(spots, state):
            value = alpha * old + gain * buf[t, level, 8 * top : 8 * top + 8, :]
            buf[t, level, 8 * top : 8 * top + 8, :] = value
            new.append(value)
        return tuple(new)

    def backward(turn, state):
        level = levels - 1 - turn
        alpha = row(coef, 0, field, level)
        gain = 1.0 - alpha
        new = []
        for (t, top), old in zip(spots, state):
            value = alpha * old + gain * buf[t, level, 8 * top : 8 * top + 8, :]
            out[level, 8 * top : 8 * top + 8, t * TILE : (t + 1) * TILE] = value
            new.append(value)
        return tuple(new)

    zeros = (splat(0.0),) * len(spots)
    lax.fori_loop(0, levels, forward, zeros, unroll=True)
    lax.fori_loop(0, levels, backward, zeros, unroll=True)


def edges(m0, m1, m2, m3, after, out):
    columns = m0.shape[2]
    near = pl.ds(pl.multiple_of((1 - lax.axis_index("gx")) * (columns - TILE), TILE), TILE)
    for k, ref in enumerate((m0, m1, m2, m3)):
        out[k] = ref[:, :, near]


def spread(m0, m1, m2, m3, after, out, work):
    columns = m0.shape[2]
    tiles = columns // TILE
    pos = position()
    for k, ref in enumerate((m0, m1, m2, m3)):
        s = pos ^ k
        for kind in range(2):
            for t in range(tiles):
                work[0, 2 * kind + s // 2, s % 2, t] = ref[kind, :, t * TILE : (t + 1) * TILE]
    for field in range(4):
        for half in range(2):
            work[0, field, half, tiles] = splat(0.0)
    diffuse(work, tiles + 1, edge_mask())
    for field in range(4):
        for half in range(2):
            for t in range(tiles):
                at = (field // 2, field % 2, slice(8 * half, 8 * half + 8), slice(t * TILE, (t + 1) * TILE))
                out[at] = work[SWEEPS % 2, field, half, t] * 0.2**SWEEPS


def finish(g0, g1, reach, bias, own, halo, latent_hbm, soft_hbm, state, work, latent, soft, sems):
    levels, columns = g0.shape[0], g0.shape[2]
    pos = position()
    keep = edge_mask()
    for k in range(GROUP):
        s = pos ^ k
        for kind in range(2):
            work[0, 2 * kind + s // 2, s % 2, 1] = halo[k, kind] * keep
            work[0, 2 * kind + s // 2, s % 2, 0] = splat(0.0)
    diffuse(work, 2, keep)
    state[...] = own[...]
    near = pl.ds(pl.multiple_of((1 - lax.axis_index("gx")) * (columns - TILE), TILE), TILE)
    for field in range(4):
        for half in range(2):
            at = (field // 2, field % 2, slice(8 * half, 8 * half + 8), near)
            state[at] += work[SWEEPS % 2, field, half, 0] * 0.2**SWEEPS
    parts = sems.shape[0]
    step = levels // parts
    tiles = columns // TILE
    copies = []
    for i in range(parts):

        def body(turn, _, i=i):
            rows = pl.ds(pl.multiple_of(8 * (turn // tiles), 8), 8)
            lanes = pl.ds(pl.multiple_of(TILE * lax.rem(turn, tiles), TILE), TILE)
            f = [state[0, field, rows, lanes] for field in range(2)]
            r = [state[1, field, rows, lanes] for field in range(2)]
            base = bias[rows, lanes]
            for level in range(i * step, (i + 1) * step):
                one = g0[level, rows, lanes] + row(reach, 0, 0, level) * f[0] + row(reach, 1, 0, level) * r[0]
                two = g1[level, rows, lanes] + row(reach, 0, 1, level) * f[1] + row(reach, 1, 1, level) * r[1]
                latent[level, 0, rows, lanes] = one
                latent[level, 1, rows, lanes] = two
                half = 0.5 + 0.5 * jnp.tanh(1.5 * (one - base))
                soft[level, rows, lanes] = half * (0.5 + 0.5 * jnp.tanh(1.5 * two))
            return 0

        lax.fori_loop(0, 2 * tiles, body, 0, unroll=True)
        at = pl.ds(i * step, step)
        copies += [
            pltpu.make_async_copy(latent.at[at], latent_hbm.at[at], sems.at[i, 0]),
            pltpu.make_async_copy(soft.at[at], soft_hbm.at[at], sems.at[i, 1]),
        ]
        for copy in copies[-2:]:
            copy.start()
    for copy in copies:
        copy.wait()


def in_hbm(value):
    return pltpu.with_memory_space_constraint(value, pltpu.HBM)


def params(mib):
    return pltpu.CompilerParams(vmem_limit_bytes=mib << 20)


def cost(flops, data):
    return pl.CostEstimate(flops=flops, bytes_accessed=data, transcendentals=0)


def xor_permute(value, axis, by):
    return lax.ppermute(value, axis, [(i, i ^ by) for i in range(lax.axis_size(axis))])


def entering_states(total, groups):
    columns = total.shape[2] - TILE
    group = lax.axis_index("gz") // GROUP

    def wide(value):
        return jnp.tile(value, (1, columns // TILE))

    def fwd(t):
        return t[0, :, :columns]

    def bwd(t):
        return t[1, :, :columns]

    if groups == 2:
        sent = jnp.where(group == 0, jnp.concatenate([total[0, :, :columns], total[0, :, columns:]], axis=1),
                         total[1])
        got = xor_permute(sent, "gz", GROUP)
        zero = jnp.zeros((8, columns), F32)
        below = got[:, :columns] + wide(got[:, columns:]) * fwd(total)
        return jnp.stack([jnp.where(group == 0, zero, got[:, :columns]), jnp.where(group == 0, below, zero)])
    size = GROUP * groups
    totals = [total]
    for turn in range(1, groups):
        totals.append(lax.ppermute(total, "gz", [(i, (i + GROUP * turn) % size) for i in range(size)]))
    stacked = jnp.stack(totals)
    state = jnp.zeros((8, columns), F32)
    f = [state]
    at = [lax.dynamic_index_in_dim(stacked, (group - j) % groups, keepdims=False) for j in range(groups)]
    for j in range(groups):
        state = wide(at[j][0, :, columns:]) * state + fwd(at[j])
        f.append(state)
    state = jnp.zeros((8, columns), F32)
    r = [None] * groups + [state]
    for j in reversed(range(groups)):
        state = bwd(at[j]) + wide(at[j][1, :, columns:]) * f[j] + wide(at[j][0, :, columns:]) * state
        r[j] = state
    return jnp.stack(
        [
            lax.dynamic_index_in_dim(jnp.stack(f[:groups]), group, keepdims=False),
            lax.dynamic_index_in_dim(jnp.stack(r[1:]), group, keepdims=False),
        ]
    )


def shards(noise, scale_index, rates, facies_code, thresholds):
    levels, _, ys, columns = noise.shape
    assert ys == 16 and levels % 8 == 0 and TILE % levels == 0 and columns * levels % (TILE * TILE) == 0
    tiles = columns // TILE
    groups = lax.axis_size("gz") // GROUP
    message = jax.ShapeDtypeStruct((2, 8, columns + TILE), F32)
    *mine, coef, packed, tiled0 = pl.pallas_call(
        carries,
        out_shape=[message] * GROUP
        + [
            jax.ShapeDtypeStruct((2, 2, levels, TILE), F32),
            jax.ShapeDtypeStruct((2, ys * levels // TILE, 8, TILE), F32),
            jax.ShapeDtypeStruct((tiles, levels, ys, TILE), F32),
        ],
        in_specs=[HBM, HBM, HBM],
        out_specs=[VMEM] * (GROUP + 3),
        scratch_shapes=[
            pltpu.VMEM((tiles, levels, ys, TILE), F32),
            pltpu.VMEM((GROUP, 2, 8, columns + TILE), F32),
            pltpu.VMEM((2, rates.shape[0], 8, TILE), F32),
            pltpu.VMEM((levels, 8, TILE), F32),
            pltpu.VMEM((2, 2, levels + 1, 8, TILE), F32),
            pltpu.SMEM((2, levels), jnp.int32),
            pltpu.SMEM(rates.shape, F32),
            pltpu.SemaphoreType.DMA((GROUP + 1, tiles)),
        ],
        compiler_params=params(50),
        cost_estimate=cost(4 * noise.size, 4 * noise.size),
        name="carries",
    )(in_hbm(scale_index.T), in_hbm(rates), in_hbm(noise))
    got = [mine[0]] + [xor_permute(mine[k], "gz", k) for k in range(1, GROUP)]
    halo = xor_permute(packed, "gx", 1)

    field_out = jax.ShapeDtypeStruct((levels, ys, columns), F32)
    field_tiled = jax.ShapeDtypeStruct((tiles, levels, ys, TILE), F32)
    scratch = [
        pltpu.VMEM((tiles, levels, ys, TILE), F32),
        pltpu.VMEM((2, ys, columns * levels // TILE + 32, TILE), F32),
    ]
    local0, tiled1 = pl.pallas_call(
        local_first,
        out_shape=[field_out, field_tiled],
        in_specs=[VMEM, VMEM, VMEM, HBM],
        out_specs=[VMEM] * 2,
        scratch_shapes=[*scratch, pltpu.SemaphoreType.DMA((tiles,))],
        compiler_params=params(45),
        cost_estimate=cost(40 * noise.size, 4 * noise.size),
        name="local0",
    )(coef, halo, tiled0, noise)
    held = pltpu.VMEM((GROUP, 2, 8, columns + TILE), F32)
    total = pl.pallas_call(
        group_total,
        out_shape=message,
        in_specs=[VMEM] * GROUP + [ANY],
        out_specs=VMEM,
        scratch_shapes=[held],
        compiler_params=params(8),
        name="group_total",
    )(*got, local0)
    reach, bias = pl.pallas_call(
        prepare,
        out_shape=[
            jax.ShapeDtypeStruct((2, 2, levels, TILE), F32),
            jax.ShapeDtypeStruct((ys, columns), F32),
        ],
        in_specs=[VMEM, VMEM, SMEM, ANY],
        out_specs=[VMEM] * 2,
        scratch_shapes=[pltpu.VMEM((levels, 8, TILE), F32)],
        compiler_params=params(4),
        cost_estimate=cost(noise.size, noise.size),
        name="prepare",
    )(coef, facies_code, thresholds, total)
    entering = entering_states(total, groups)
    state = jax.ShapeDtypeStruct((2, 8, columns), F32)
    own = pl.pallas_call(
        enter_group,
        out_shape=[state] * GROUP,
        in_specs=[VMEM] * (GROUP + 1) + [ANY],
        out_specs=[VMEM] * GROUP,
        scratch_shapes=[held],
        compiler_params=params(8),
        name="enter_group",
    )(*got, entering, reach)
    states = [own[0]] + [xor_permute(own[k], "gz", k) for k in range(1, GROUP)]
    local1 = pl.pallas_call(
        functools.partial(local_field, 1),
        out_shape=field_out,
        in_specs=[VMEM, VMEM, VMEM, ANY],
        out_specs=VMEM,
        scratch_shapes=scratch,
        compiler_params=params(16),
        cost_estimate=cost(40 * noise.size, 4 * noise.size),
        name="local1",
    )(coef, halo, tiled1, own[0])
    near = pl.pallas_call(
        edges,
        out_shape=jax.ShapeDtypeStruct((GROUP, 2, 8, TILE), F32),
        in_specs=[VMEM] * GROUP + [ANY],
        out_specs=VMEM,
        compiler_params=params(4),
        name="edges",
    )(*states, local1)
    spread_out = pl.pallas_call(
        spread,
        out_shape=jax.ShapeDtypeStruct((2, 2, ys, columns), F32),
        in_specs=[VMEM] * GROUP + [ANY],
        out_specs=VMEM,
        scratch_shapes=[pltpu.VMEM((2, 4, 2, tiles + 1, 8, TILE), F32)],
        compiler_params=params(8),
        cost_estimate=cost(4 * noise.size, noise.size),
        name="spread",
    )(*states, near)
    near = xor_permute(near, "gx", 1)
    out = [
        jax.ShapeDtypeStruct(noise.shape, F32),
        jax.ShapeDtypeStruct((levels, ys, columns), F32),
    ]
    latent, soft = pl.pallas_call(
        finish,
        out_shape=out,
        in_specs=[VMEM] * 6,
        out_specs=[ANY, ANY],
        scratch_shapes=[
            pltpu.VMEM((2, 2, ys, columns), F32),
            pltpu.VMEM((2, 4, 2, 2, 8, TILE), F32),
            pltpu.VMEM(noise.shape, F32),
            pltpu.VMEM((levels, ys, columns), F32),
            pltpu.SemaphoreType.DMA((8, 2)),
        ],
        compiler_params=params(24),
        name="finish",
    )(local0, local1, reach, bias, spread_out, near)
    return latent, soft


def solution(mesh):
    return jax.shard_map(
        shards,
        mesh=mesh,
        in_specs=(
            P(("parts", "gz"), None, None, "gx"),
            P(("parts", "gz"), None),
            P(),
            P("parts", "gx"),
            P(),
        ),
        out_specs=(P(("parts", "gz"), None, None, "gx"), P(("parts", "gz"), None, "gx")),
        check_vma=False,
    )
```

```python
import functools

import jax
import jax.numpy as jnp
from jax import lax
from jax.experimental import pallas as pl
from jax.experimental.pallas import tpu as pltpu
from jax.sharding import PartitionSpec as P

SWEEPS = 4
GROUP = 4
TILE = 128
F32 = jnp.float32
SMEM = pl.BlockSpec(memory_space=pltpu.SMEM)
ANY = pl.BlockSpec(memory_space=pl.ANY)
VMEM = pl.BlockSpec(memory_space=pltpu.VMEM)
HBM = pl.BlockSpec(memory_space=pltpu.HBM)


def splat(value):
    return jnp.full((8, TILE), value, F32)


def row(ref, *at):
    return jnp.broadcast_to(ref[(*at[:-1], pl.ds(at[-1], 1), slice(None))], (8, TILE))


def fill_tables(rates, table):
    for i in range(rates.shape[0]):
        alpha = jnp.exp(-splat(rates[i]))
        table[0, i] = alpha
        table[1, i] = jnp.sqrt(1.0 - alpha * alpha)


def position():
    return lax.rem(lax.axis_index("gz"), GROUP)


def carries(idx_hbm, rates_hbm, noise_hbm, out0, out1, out2, out3, coef, packed, tiled0, tiled1, held, table, pre, wts, idx, rates, sems):
    outs, tiled = (out0, out1, out2, out3), (tiled0, tiled1)
    levels, columns = noise_hbm.shape[0], noise_hbm.shape[3]
    tiles = columns // TILE
    pos = position()
    core = lax.axis_index("gx")
    small = [
        pltpu.make_async_copy(idx_hbm, idx, sems.at[GROUP, 0]),
        pltpu.make_async_copy(rates_hbm, rates, sems.at[GROUP, 1]),
    ]
    for copy in small:
        copy.start()
    copies = []
    for s in range(GROUP):
        rows = slice(8 * (s % 2), 8 * (s % 2) + 8)
        copies.append([])
        for t in range(tiles):
            source = noise_hbm.at[:, s // 2, rows, pl.ds(t * TILE, TILE)]
            copies[s].append(pltpu.make_async_copy(source, tiled[s // 2].at[t, :, rows, :], sems.at[s, t]))
            copies[s][t].start()
    for copy in small:
        copy.wait()
    fill_tables(rates, table)
    for field in range(2):
        run = splat(1.0)
        for k in range(levels):
            pre[k] = run
            run = run * table[0, idx[field, k]]
        total = run
        post, gather, after = splat(1.0), splat(0.0), splat(0.0)
        for k in reversed(range(levels)):
            alpha, gain = table[0, idx[field, k]], table[1, idx[field, k]]
            coef[0, field, k : k + 1, :] = alpha[:1]
            coef[1, field, k : k + 1, :] = gain[:1]
            gather = pre[k] * (1.0 - alpha) + after * gather
            wts[0, field, k] = gain * post
            wts[1, field, k] = gain * gather
            post = post * alpha
            after = alpha
        wts[0, field, levels] = total
        wts[1, field, levels] = after * gather
    near = (1 - core) * (tiles - 1)
    for s in range(GROUP):
        for copy in copies[s]:
            copy.wait()
        field, k = s // 2, pos ^ s
        rows = slice(8 * (s % 2), 8 * (s % 2) + 8)
        for half in range(2):
            ours = range(half * tiles // 2, (half + 1) * tiles // 2)

            def body(level, sums, field=field, rows=rows, ours=ours):
                fwd, bwd = wts[0, field, level], wts[1, field, level]
                new = []
                for t, (one, two) in zip(ours, sums):
                    value = tiled[field][t, level, rows, :]
                    new.append((one + fwd * value, two + bwd * value))
                return tuple(new)

            sums = lax.fori_loop(0, levels, body, ((splat(0.0), splat(0.0)),) * len(ours), unroll=True)
            for t, (one, two) in zip(ours, sums):
                held[k, 0, :, t * TILE : (t + 1) * TILE] = one
                held[k, 1, :, t * TILE : (t + 1) * TILE] = two
        held[k, 0, :, columns:] = wts[0, field, levels]
        held[k, 1, :, columns:] = wts[1, field, levels]
        if s % 2 == 0:
            continue
        flat = tiled[field].reshape(tiles, levels * 16, TILE)
        for first in range(0, 16, TILE // levels):
            parts = [
                flat[near, pl.ds(8 * g * 16 + y, 8, stride=16), :]
                for y in range(first, first + TILE // levels)
                for g in range(levels // 8)
            ]
            turned = jnp.concatenate(parts, axis=0).T
            packed[field, first * levels // TILE] = jnp.where(core == 0, turned[TILE - 8 :], turned[:8])
    for k in range(GROUP):
        outs[k][...] = held[k]


def scan_group(held, lanes, f_in, r_in):
    columns = held.shape[3] - TILE
    f = [f_in]
    for j in range(GROUP):
        f.append(held[j, 0, :, columns:] * f[j] + held[j, 0, :, lanes])
    r = [None] * GROUP + [r_in]
    for j in reversed(range(GROUP)):
        r[j] = held[j, 1, :, lanes] + held[j, 1, :, columns:] * f[j] + held[j, 0, :, columns:] * r[j + 1]
    return f, r


def hold(refs, held):
    pos = position()
    for k, ref in enumerate(refs):
        held[pos ^ k] = ref[...]


def group_total(m0, m1, m2, m3, after, out, held):
    hold((m0, m1, m2, m3), held)
    columns = held.shape[3] - TILE
    zero = splat(0.0)
    for t in range(columns // TILE):
        lanes = slice(t * TILE, (t + 1) * TILE)
        f, r = scan_group(held, lanes, zero, zero)
        out[0, :, lanes] = f[GROUP]
        out[1, :, lanes] = r[0]
    run, factor = splat(1.0), splat(0.0)
    for j in range(GROUP):
        run = run * held[j, 0, :, columns:]
    for j in reversed(range(GROUP)):
        a, c = held[j, 0, :, columns:], held[j, 1, :, columns:]
        factor = c + a * a * factor
    out[0, :, columns:] = run
    out[1, :, columns:] = factor


def enter_group(m0, m1, m2, m3, entering, after, out0, out1, out2, out3, held):
    hold((m0, m1, m2, m3), held)
    columns = held.shape[3] - TILE
    outs = (out0, out1, out2, out3)
    pos = position()
    for t in range(columns // TILE):
        lanes = slice(t * TILE, (t + 1) * TILE)
        f, r = scan_group(held, lanes, entering[0, :, lanes], entering[1, :, lanes])
        for j in range(GROUP):
            held[j, 0, :, lanes] = f[j]
            held[j, 1, :, lanes] = r[j + 1]
    for k in range(GROUP):
        outs[k][...] = held[pos ^ k, :, :, :columns]


def diffuse(work, tiles, keep):
    fields = work.shape[1]
    lane = lax.broadcasted_iota(jnp.int32, (8, TILE), 1)
    line = lax.broadcasted_iota(jnp.int32, (8, TILE), 0)
    for turn in range(SWEEPS):
        src, dst = turn % 2, 1 - turn % 2
        for field in range(fields):
            for t in range(tiles):
                pair = [work[src, field, half, t] for half in range(2)]
                above = [pltpu.roll(v, 1, 0) for v in pair]
                below = [pltpu.roll(v, 7, 0) for v in pair]
                above = [jnp.where(line == 0, 0.0, above[0]), jnp.where(line == 0, above[0], above[1])]
                below = [jnp.where(line == 7, below[1], below[0]), jnp.where(line == 7, 0.0, below[1])]
                for half, value in enumerate(pair):
                    before = work[src, field, half, (t - 1) % tiles]
                    later = work[src, field, half, (t + 1) % tiles]
                    side = pltpu.roll(jnp.where(lane == TILE - 1, before, value), 1, 1)
                    side += pltpu.roll(jnp.where(lane == 0, later, value), TILE - 1, 1)
                    new = value + side + (above[half] + below[half])
                    work[dst, field, half, t] = new * keep if t == tiles - 1 else new


def edge_mask():
    lane = lax.broadcasted_iota(jnp.int32, (8, TILE), 1)
    core = lax.axis_index("gx")
    return ((lane < TILE // 2) == (core == 0)).astype(F32)


def prepare(coef, codes, thresholds, after, reach, bias, pre):
    levels = coef.shape[2]
    for field in range(2):
        run = splat(1.0)
        for k in range(levels):
            run = run * row(coef, 0, field, k)
            pre[k] = run
        down, up = splat(0.0), splat(1.0)
        for k in reversed(range(levels)):
            alpha = row(coef, 0, field, k)
            down = alpha * down + (1.0 - alpha) * pre[k]
            up = alpha * up
            reach[0, field, k : k + 1, :] = down[:1]
            reach[1, field, k : k + 1, :] = up[:1]
    code = codes[...]
    value = jnp.zeros(code.shape, F32)
    for i in range(thresholds.shape[0]):
        value = jnp.where(code == i, thresholds[i], value)
    bias[...] = value


def sweep_first(packed, tiled, noise_hbm, buf, tiled_next, work, sems):
    copies = [
        pltpu.make_async_copy(noise_hbm.at[:, 1, :, pl.ds(t * TILE, TILE)], tiled_next.at[t], sems.at[t])
        for t in range(tiled.shape[0])
    ]
    for copy in copies:
        copy.start()
    sweep_field(0, packed, tiled, buf, work)
    for copy in copies:
        copy.wait()


def sweep_field(field, packed, tiled, buf, work):
    tiles, levels, ys, _ = tiled.shape
    columns = tiles * TILE
    ranges = TILE // levels
    span = columns // ranges
    blocks = span // TILE
    main = 16
    core = lax.axis_index("gx")
    lane = lax.broadcasted_iota(jnp.int32, (8, TILE), 1)
    keep_left = (lane >= levels) | (core == 1)
    keep_right = (lane < TILE - levels) | (core == 0)
    source = tiled.reshape(tiles, levels * ys, TILE)
    flat = buf.reshape(tiles, levels * ys, TILE)
    for slot in range(2):
        for y in range(ys):
            work[slot, y, 0:8, :] = splat(0.0)
            work[slot, y, main + span + 8 :, :] = splat(0.0)

    def pieces(y):
        return [(c, g, pl.ds(8 * g * ys + y, 8, stride=ys)) for c in range(ranges) for g in range(levels // 8)]

    for y in range(ys):
        for b in range(blocks):
            rows = [source[c * blocks + b, at, :] for c, g, at in pieces(y)]
            work[0, y, main + b * TILE : main + (b + 1) * TILE, :] = jnp.concatenate(rows, axis=0).T
        edge, place = packed[field, y // ranges], y % ranges
        left = pltpu.roll(work[0, y, main + span - 8 : main + span, :], levels, 1)
        right = pltpu.roll(work[0, y, main : main + 8, :], TILE - levels, 1)
        far_left = pltpu.roll(edge, (TILE - levels * place) % TILE, 1)
        far_right = pltpu.roll(edge, levels * (ranges - 1 - place), 1)
        left = jnp.where(keep_left, jnp.where(lane < levels, far_left, left), 0.0)
        right = jnp.where(keep_right, jnp.where(lane >= TILE - levels, far_right, right), 0.0)
        work[0, y, main - 8 : main, :] = left
        work[0, y, main + span : main + span + 8, :] = right

    def block(src, at, before, later, keep=None):
        above, here = splat(0.0), work[src, 0, at, :]
        for y in range(ys):
            below = work[src, y + 1, at, :] if y + 1 < ys else splat(0.0)
            new = here + (work[src, y, before, :] + work[src, y, later, :]) + (above + below)
            if keep is not None:
                new = jnp.where(keep, new, 0.0)
            work[1 - src, y, at, :] = new
            above, here = here, below

    for turn in range(SWEEPS):
        src = turn % 2

        def step(r, _, src=src):
            at = pl.multiple_of(main + 8 * r, 8)
            block(src, pl.ds(at, 8), pl.ds(at - 1, 8), pl.ds(at + 1, 8))
            return 0

        lax.fori_loop(0, span // 8, step, 0, unroll=True)
        if turn + 1 < SWEEPS:
            for at, keep in ((main - 8, keep_left), (main + span, keep_right)):
                block(src, pl.ds(at, 8), pl.ds(at - 1, 8), pl.ds(at + 1, 8), keep)
    for y in range(ys):
        for b in range(blocks):
            turned = work[SWEEPS % 2, y, main + b * TILE : main + (b + 1) * TILE, :].T
            for i, (c, g, at) in enumerate(pieces(y)):
                flat[c * blocks + b, at, :] = turned[8 * i : 8 * i + 8]


def filter_first(coef, mixed, after, out, buf):
    filter_field(0, coef, mixed, buf, out)


def local_field(field, coef, packed, tiled, after, out, buf, work):
    sweep_field(field, packed, tiled, buf, work)
    filter_field(field, coef, buf, buf, out)


def filter_field(field, coef, mixed, buf, out):
    tiles, levels, ys, _ = mixed.shape
    scale = 0.2**SWEEPS
    spots = [(t, top) for t in range(tiles) for top in range(ys // 8)]

    def forward(level, state):
        alpha, gain = row(coef, 0, field, level), row(coef, 1, field, level) * scale
        new = []
        for (t, top), old in zip(spots, state):
            value = alpha * old + gain * mixed[t, level, 8 * top : 8 * top + 8, :]
            buf[t, level, 8 * top : 8 * top + 8, :] = value
            new.append(value)
        return tuple(new)

    def backward(turn, state):
        level = levels - 1 - turn
        alpha = row(coef, 0, field, level)
        gain = 1.0 - alpha
        new = []
        for (t, top), old in zip(spots, state):
            value = alpha * old + gain * buf[t, level, 8 * top : 8 * top + 8, :]
            out[level, 8 * top : 8 * top + 8, t * TILE : (t + 1) * TILE] = value
            new.append(value)
        return tuple(new)

    zeros = (splat(0.0),) * len(spots)
    lax.fori_loop(0, levels, forward, zeros, unroll=True)
    lax.fori_loop(0, levels, backward, zeros, unroll=True)


def edges(m0, m1, m2, m3, after, out):
    columns = m0.shape[2]
    near = pl.ds(pl.multiple_of((1 - lax.axis_index("gx")) * (columns - TILE), TILE), TILE)
    for k, ref in enumerate((m0, m1, m2, m3)):
        out[k] = ref[:, :, near]


def spread(m0, m1, m2, m3, after, out, work):
    columns = m0.shape[2]
    tiles = columns // TILE
    pos = position()
    for k, ref in enumerate((m0, m1, m2, m3)):
        s = pos ^ k
        for kind in range(2):
            for t in range(tiles):
                work[0, 2 * kind + s // 2, s % 2, t] = ref[kind, :, t * TILE : (t + 1) * TILE]
    for field in range(4):
        for half in range(2):
            work[0, field, half, tiles] = splat(0.0)
    diffuse(work, tiles + 1, edge_mask())
    for field in range(4):
        for half in range(2):
            for t in range(tiles):
                at = (field // 2, field % 2, slice(8 * half, 8 * half + 8), slice(t * TILE, (t + 1) * TILE))
                out[at] = work[SWEEPS % 2, field, half, t] * 0.2**SWEEPS


def finish(g0, g1, reach, bias, own, halo, latent_hbm, soft_hbm, state, work, latent, soft, sems):
    levels, columns = g0.shape[0], g0.shape[2]
    pos = position()
    keep = edge_mask()
    for k in range(GROUP):
        s = pos ^ k
        for kind in range(2):
            work[0, 2 * kind + s // 2, s % 2, 1] = halo[k, kind] * keep
            work[0, 2 * kind + s // 2, s % 2, 0] = splat(0.0)
    diffuse(work, 2, keep)
    state[...] = own[...]
    near = pl.ds(pl.multiple_of((1 - lax.axis_index("gx")) * (columns - TILE), TILE), TILE)
    for field in range(4):
        for half in range(2):
            at = (field // 2, field % 2, slice(8 * half, 8 * half + 8), near)
            state[at] += work[SWEEPS % 2, field, half, 0] * 0.2**SWEEPS
    parts = sems.shape[0]
    step = levels // parts
    tiles = columns // TILE
    copies = []
    for i in range(parts):

        def body(turn, _, i=i):
            rows = pl.ds(pl.multiple_of(8 * (turn // tiles), 8), 8)
            lanes = pl.ds(pl.multiple_of(TILE * lax.rem(turn, tiles), TILE), TILE)
            f = [state[0, field, rows, lanes] for field in range(2)]
            r = [state[1, field, rows, lanes] for field in range(2)]
            base = bias[rows, lanes]
            for level in range(i * step, (i + 1) * step):
                one = g0[level, rows, lanes] + row(reach, 0, 0, level) * f[0] + row(reach, 1, 0, level) * r[0]
                two = g1[level, rows, lanes] + row(reach, 0, 1, level) * f[1] + row(reach, 1, 1, level) * r[1]
                latent[level, 0, rows, lanes] = one
                latent[level, 1, rows, lanes] = two
                half = 0.5 + 0.5 * jnp.tanh(1.5 * (one - base))
                soft[level, rows, lanes] = half * (0.5 + 0.5 * jnp.tanh(1.5 * two))
            return 0

        lax.fori_loop(0, 2 * tiles, body, 0, unroll=True)
        at = pl.ds(i * step, step)
        copies += [
            pltpu.make_async_copy(latent.at[at], latent_hbm.at[at], sems.at[i, 0]),
            pltpu.make_async_copy(soft.at[at], soft_hbm.at[at], sems.at[i, 1]),
        ]
        for copy in copies[-2:]:
            copy.start()
    for copy in copies:
        copy.wait()


def in_hbm(value):
    return pltpu.with_memory_space_constraint(value, pltpu.HBM)


def params(mib):
    return pltpu.CompilerParams(vmem_limit_bytes=mib << 20)


def cost(flops, data):
    return pl.CostEstimate(flops=flops, bytes_accessed=data, transcendentals=0)


def xor_permute(value, axis, by):
    return lax.ppermute(value, axis, [(i, i ^ by) for i in range(lax.axis_size(axis))])


def entering_states(total, groups):
    columns = total.shape[2] - TILE
    group = lax.axis_index("gz") // GROUP

    def wide(value):
        return jnp.tile(value, (1, columns // TILE))

    def fwd(t):
        return t[0, :, :columns]

    def bwd(t):
        return t[1, :, :columns]

    if groups == 2:
        sent = jnp.where(group == 0, jnp.concatenate([total[0, :, :columns], total[0, :, columns:]], axis=1),
                         total[1])
        got = xor_permute(sent, "gz", GROUP)
        zero = jnp.zeros((8, columns), F32)
        below = got[:, :columns] + wide(got[:, columns:]) * fwd(total)
        return jnp.stack([jnp.where(group == 0, zero, got[:, :columns]), jnp.where(group == 0, below, zero)])
    size = GROUP * groups
    totals = [total]
    for turn in range(1, groups):
        totals.append(lax.ppermute(total, "gz", [(i, (i + GROUP * turn) % size) for i in range(size)]))
    stacked = jnp.stack(totals)
    state = jnp.zeros((8, columns), F32)
    f = [state]
    at = [lax.dynamic_index_in_dim(stacked, (group - j) % groups, keepdims=False) for j in range(groups)]
    for j in range(groups):
        state = wide(at[j][0, :, columns:]) * state + fwd(at[j])
        f.append(state)
    state = jnp.zeros((8, columns), F32)
    r = [None] * groups + [state]
    for j in reversed(range(groups)):
        state = bwd(at[j]) + wide(at[j][1, :, columns:]) * f[j] + wide(at[j][0, :, columns:]) * state
        r[j] = state
    return jnp.stack(
        [
            lax.dynamic_index_in_dim(jnp.stack(f[:groups]), group, keepdims=False),
            lax.dynamic_index_in_dim(jnp.stack(r[1:]), group, keepdims=False),
        ]
    )


def shards(noise, scale_index, rates, facies_code, thresholds):
    levels, _, ys, columns = noise.shape
    assert ys == 16 and levels % 8 == 0 and TILE % levels == 0 and columns * levels % (TILE * TILE) == 0
    tiles = columns // TILE
    groups = lax.axis_size("gz") // GROUP
    message = jax.ShapeDtypeStruct((2, 8, columns + TILE), F32)
    *mine, coef, packed, tiled0 = pl.pallas_call(
        carries,
        out_shape=[message] * GROUP
        + [
            jax.ShapeDtypeStruct((2, 2, levels, TILE), F32),
            jax.ShapeDtypeStruct((2, ys * levels // TILE, 8, TILE), F32),
            jax.ShapeDtypeStruct((tiles, levels, ys, TILE), F32),
        ],
        in_specs=[HBM, HBM, HBM],
        out_specs=[VMEM] * (GROUP + 3),
        scratch_shapes=[
            pltpu.VMEM((tiles, levels, ys, TILE), F32),
            pltpu.VMEM((GROUP, 2, 8, columns + TILE), F32),
            pltpu.VMEM((2, rates.shape[0], 8, TILE), F32),
            pltpu.VMEM((levels, 8, TILE), F32),
            pltpu.VMEM((2, 2, levels + 1, 8, TILE), F32),
            pltpu.SMEM((2, levels), jnp.int32),
            pltpu.SMEM(rates.shape, F32),
            pltpu.SemaphoreType.DMA((GROUP + 1, tiles)),
        ],
        compiler_params=params(50),
        cost_estimate=cost(4 * noise.size, 4 * noise.size),
        name="carries",
    )(in_hbm(scale_index.T), in_hbm(rates), in_hbm(noise))
    got = [mine[0]] + [xor_permute(mine[k], "gz", k) for k in range(1, GROUP)]
    halo = xor_permute(packed, "gx", 1)

    field_out = jax.ShapeDtypeStruct((levels, ys, columns), F32)
    field_tiled = jax.ShapeDtypeStruct((tiles, levels, ys, TILE), F32)
    scratch = [
        pltpu.VMEM((tiles, levels, ys, TILE), F32),
        pltpu.VMEM((2, ys, columns * levels // TILE + 32, TILE), F32),
    ]
    mixed, tiled1 = pl.pallas_call(
        sweep_first,
        out_shape=[field_tiled] * 2,
        in_specs=[VMEM, VMEM, HBM],
        out_specs=[VMEM] * 2,
        scratch_shapes=[scratch[1], pltpu.SemaphoreType.DMA((tiles,))],
        compiler_params=params(45),
        cost_estimate=cost(40 * noise.size, 4 * noise.size),
        name="sweep0",
    )(halo, tiled0, in_hbm(noise))
    held = pltpu.VMEM((GROUP, 2, 8, columns + TILE), F32)
    total = pl.pallas_call(
        group_total,
        out_shape=message,
        in_specs=[VMEM] * GROUP + [ANY],
        out_specs=VMEM,
        scratch_shapes=[held],
        compiler_params=params(8),
        name="group_total",
    )(*got, mixed)
    local0 = pl.pallas_call(
        filter_first,
        out_shape=field_out,
        in_specs=[VMEM, VMEM, ANY],
        out_specs=VMEM,
        scratch_shapes=[scratch[0]],
        compiler_params=params(16),
        cost_estimate=cost(8 * noise.size, noise.size),
        name="filter0",
    )(coef, mixed, total)
    reach, bias = pl.pallas_call(
        prepare,
        out_shape=[
            jax.ShapeDtypeStruct((2, 2, levels, TILE), F32),
            jax.ShapeDtypeStruct((ys, columns), F32),
        ],
        in_specs=[VMEM, VMEM, SMEM, ANY],
        out_specs=[VMEM] * 2,
        scratch_shapes=[pltpu.VMEM((levels, 8, TILE), F32)],
        compiler_params=params(4),
        cost_estimate=cost(noise.size, noise.size),
        name="prepare",
    )(coef, facies_code, thresholds, local0)
    entering = entering_states(total, groups)
    state = jax.ShapeDtypeStruct((2, 8, columns), F32)
    own = pl.pallas_call(
        enter_group,
        out_shape=[state] * GROUP,
        in_specs=[VMEM] * (GROUP + 1) + [ANY],
        out_specs=[VMEM] * GROUP,
        scratch_shapes=[held],
        compiler_params=params(8),
        name="enter_group",
    )(*got, entering, reach)
    states = [own[0]] + [xor_permute(own[k], "gz", k) for k in range(1, GROUP)]
    local1 = pl.pallas_call(
        functools.partial(local_field, 1),
        out_shape=field_out,
        in_specs=[VMEM, VMEM, VMEM, ANY],
        out_specs=VMEM,
        scratch_shapes=scratch,
        compiler_params=params(16),
        cost_estimate=cost(40 * noise.size, 4 * noise.size),
        name="local1",
    )(coef, halo, tiled1, own[0])
    near = pl.pallas_call(
        edges,
        out_shape=jax.ShapeDtypeStruct((GROUP, 2, 8, TILE), F32),
        in_specs=[VMEM] * GROUP + [ANY],
        out_specs=VMEM,
        compiler_params=params(4),
        name="edges",
    )(*states, local1)
    spread_out = pl.pallas_call(
        spread,
        out_shape=jax.ShapeDtypeStruct((2, 2, ys, columns), F32),
        in_specs=[VMEM] * GROUP + [ANY],
        out_specs=VMEM,
        scratch_shapes=[pltpu.VMEM((2, 4, 2, tiles + 1, 8, TILE), F32)],
        compiler_params=params(8),
        cost_estimate=cost(4 * noise.size, noise.size),
        name="spread",
    )(*states, near)
    near = xor_permute(near, "gx", 1)
    out = [
        jax.ShapeDtypeStruct(noise.shape, F32),
        jax.ShapeDtypeStruct((levels, ys, columns), F32),
    ]
    latent, soft = pl.pallas_call(
        finish,
        out_shape=out,
        in_specs=[VMEM] * 6,
        out_specs=[ANY, ANY],
        scratch_shapes=[
            pltpu.VMEM((2, 2, ys, columns), F32),
            pltpu.VMEM((2, 4, 2, 2, 8, TILE), F32),
            pltpu.VMEM(noise.shape, F32),
            pltpu.VMEM((levels, ys, columns), F32),
            pltpu.SemaphoreType.DMA((8, 2)),
        ],
        compiler_params=params(24),
        name="finish",
    )(local0, local1, reach, bias, spread_out, near)
    return latent, soft


def solution(mesh):
    return jax.shard_map(
        shards,
        mesh=mesh,
        in_specs=(
            P(("parts", "gz"), None, None, "gx"),
            P(("parts", "gz"), None),
            P(),
            P("parts", "gx"),
            P(),
        ),
        out_specs=(P(("parts", "gz"), None, None, "gx"), P(("parts", "gz"), None, "gx")),
        check_vma=False,
    )
```

```python
import functools

import jax
import jax.numpy as jnp
from jax import lax
from jax.experimental import pallas as pl
from jax.experimental.pallas import tpu as pltpu
from jax.sharding import PartitionSpec as P

SWEEPS = 4
GROUP = 4
TILE = 128
F32 = jnp.float32
SMEM = pl.BlockSpec(memory_space=pltpu.SMEM)
ANY = pl.BlockSpec(memory_space=pl.ANY)
VMEM = pl.BlockSpec(memory_space=pltpu.VMEM)
HBM = pl.BlockSpec(memory_space=pltpu.HBM)


def splat(value):
    return jnp.full((8, TILE), value, F32)


def row(ref, *at):
    return jnp.broadcast_to(ref[(*at[:-1], pl.ds(at[-1], 1), slice(None))], (8, TILE))


def fill_tables(rates, table):
    for i in range(rates.shape[0]):
        alpha = jnp.exp(-splat(rates[i]))
        table[0, i] = alpha
        table[1, i] = jnp.sqrt(1.0 - alpha * alpha)


def position():
    return lax.rem(lax.axis_index("gz"), GROUP)


def carries(idx_hbm, rates_hbm, noise_hbm, out0, out1, out2, out3, coef, packed, tiled0, tiled1, held, table, pre, wts, idx, rates, sems):
    outs, tiled = (out0, out1, out2, out3), (tiled0, tiled1)
    levels, columns = noise_hbm.shape[0], noise_hbm.shape[3]
    tiles = columns // TILE
    pos = position()
    core = lax.axis_index("gx")
    small = [
        pltpu.make_async_copy(idx_hbm, idx, sems.at[GROUP, 0]),
        pltpu.make_async_copy(rates_hbm, rates, sems.at[GROUP, 1]),
    ]
    for copy in small:
        copy.start()
    copies = []
    for s in range(GROUP):
        rows = slice(8 * (s % 2), 8 * (s % 2) + 8)
        copies.append([])
        for t in range(tiles):
            source = noise_hbm.at[:, s // 2, rows, pl.ds(t * TILE, TILE)]
            copies[s].append(pltpu.make_async_copy(source, tiled[s // 2].at[t, :, rows, :], sems.at[s, t]))
            copies[s][t].start()
    for copy in small:
        copy.wait()
    fill_tables(rates, table)
    for field in range(2):
        run = splat(1.0)
        for k in range(levels):
            pre[k] = run
            run = run * table[0, idx[field, k]]
        total = run
        post, gather, after = splat(1.0), splat(0.0), splat(0.0)
        for k in reversed(range(levels)):
            alpha, gain = table[0, idx[field, k]], table[1, idx[field, k]]
            coef[0, field, k : k + 1, :] = alpha[:1]
            coef[1, field, k : k + 1, :] = gain[:1]
            gather = pre[k] * (1.0 - alpha) + after * gather
            wts[0, field, k] = gain * post
            wts[1, field, k] = gain * gather
            post = post * alpha
            after = alpha
        wts[0, field, levels] = total
        wts[1, field, levels] = after * gather
    near = (1 - core) * (tiles - 1)
    for s in range(GROUP):
        for copy in copies[s]:
            copy.wait()
        field, k = s // 2, pos ^ s
        rows = slice(8 * (s % 2), 8 * (s % 2) + 8)
        for half in range(2):
            ours = range(half * tiles // 2, (half + 1) * tiles // 2)

            def body(level, sums, field=field, rows=rows, ours=ours):
                fwd, bwd = wts[0, field, level], wts[1, field, level]
                new = []
                for t, (one, two) in zip(ours, sums):
                    value = tiled[field][t, level, rows, :]
                    new.append((one + fwd * value, two + bwd * value))
                return tuple(new)

            sums = lax.fori_loop(0, levels, body, ((splat(0.0), splat(0.0)),) * len(ours), unroll=True)
            for t, (one, two) in zip(ours, sums):
                held[k, 0, :, t * TILE : (t + 1) * TILE] = one
                held[k, 1, :, t * TILE : (t + 1) * TILE] = two
        held[k, 0, :, columns:] = wts[0, field, levels]
        held[k, 1, :, columns:] = wts[1, field, levels]
        if s % 2 == 0:
            continue
        flat = tiled[field].reshape(tiles, levels * 16, TILE)
        for first in range(0, 16, TILE // levels):
            parts = [
                flat[near, pl.ds(8 * g * 16 + y, 8, stride=16), :]
                for y in range(first, first + TILE // levels)
                for g in range(levels // 8)
            ]
            turned = jnp.concatenate(parts, axis=0).T
            packed[field, first * levels // TILE] = jnp.where(core == 0, turned[TILE - 8 :], turned[:8])
    for k in range(GROUP):
        outs[k][...] = held[k]


def scan_group(held, lanes, f_in, r_in):
    columns = held.shape[3] - TILE
    f = [f_in]
    for j in range(GROUP):
        f.append(held[j, 0, :, columns:] * f[j] + held[j, 0, :, lanes])
    r = [None] * GROUP + [r_in]
    for j in reversed(range(GROUP)):
        r[j] = held[j, 1, :, lanes] + held[j, 1, :, columns:] * f[j] + held[j, 0, :, columns:] * r[j + 1]
    return f, r


def hold(refs, held):
    pos = position()
    for k, ref in enumerate(refs):
        held[pos ^ k] = ref[...]


def group_total(m0, m1, m2, m3, after, out, held):
    hold((m0, m1, m2, m3), held)
    columns = held.shape[3] - TILE
    zero = splat(0.0)
    for t in range(columns // TILE):
        lanes = slice(t * TILE, (t + 1) * TILE)
        f, r = scan_group(held, lanes, zero, zero)
        out[0, :, lanes] = f[GROUP]
        out[1, :, lanes] = r[0]
    run, factor = splat(1.0), splat(0.0)
    for j in range(GROUP):
        run = run * held[j, 0, :, columns:]
    for j in reversed(range(GROUP)):
        a, c = held[j, 0, :, columns:], held[j, 1, :, columns:]
        factor = c + a * a * factor
    out[0, :, columns:] = run
    out[1, :, columns:] = factor


def enter_group(m0, m1, m2, m3, entering, after, out0, out1, out2, out3, held):
    hold((m0, m1, m2, m3), held)
    columns = held.shape[3] - TILE
    outs = (out0, out1, out2, out3)
    pos = position()
    for t in range(columns // TILE):
        lanes = slice(t * TILE, (t + 1) * TILE)
        f, r = scan_group(held, lanes, entering[0, :, lanes], entering[1, :, lanes])
        for j in range(GROUP):
            held[j, 0, :, lanes] = f[j]
            held[j, 1, :, lanes] = r[j + 1]
    for k in range(GROUP):
        outs[k][...] = held[pos ^ k, :, :, :columns]


def diffuse(work, tiles, keep):
    fields = work.shape[1]
    lane = lax.broadcasted_iota(jnp.int32, (8, TILE), 1)
    line = lax.broadcasted_iota(jnp.int32, (8, TILE), 0)
    for turn in range(SWEEPS):
        src, dst = turn % 2, 1 - turn % 2
        for field in range(fields):
            for t in range(tiles):
                pair = [work[src, field, half, t] for half in range(2)]
                above = [pltpu.roll(v, 1, 0) for v in pair]
                below = [pltpu.roll(v, 7, 0) for v in pair]
                above = [jnp.where(line == 0, 0.0, above[0]), jnp.where(line == 0, above[0], above[1])]
                below = [jnp.where(line == 7, below[1], below[0]), jnp.where(line == 7, 0.0, below[1])]
                for half, value in enumerate(pair):
                    before = work[src, field, half, (t - 1) % tiles]
                    later = work[src, field, half, (t + 1) % tiles]
                    side = pltpu.roll(jnp.where(lane == TILE - 1, before, value), 1, 1)
                    side += pltpu.roll(jnp.where(lane == 0, later, value), TILE - 1, 1)
                    new = value + side + (above[half] + below[half])
                    work[dst, field, half, t] = new * keep if t == tiles - 1 else new


def edge_mask():
    lane = lax.broadcasted_iota(jnp.int32, (8, TILE), 1)
    core = lax.axis_index("gx")
    return ((lane < TILE // 2) == (core == 0)).astype(F32)


def prepare(coef, codes, thresholds, after, reach, bias, pre):
    levels = coef.shape[2]
    for field in range(2):
        run = splat(1.0)
        for k in range(levels):
            run = run * row(coef, 0, field, k)
            pre[k] = run
        down, up = splat(0.0), splat(1.0)
        for k in reversed(range(levels)):
            alpha = row(coef, 0, field, k)
            down = alpha * down + (1.0 - alpha) * pre[k]
            up = alpha * up
            reach[0, field, k : k + 1, :] = down[:1]
            reach[1, field, k : k + 1, :] = up[:1]
    code = codes[...]
    value = jnp.zeros(code.shape, F32)
    for i in range(thresholds.shape[0]):
        value = jnp.where(code == i, thresholds[i], value)
    bias[...] = value


def sweep_first(packed, tiled, noise_hbm, buf, tiled_next, work, sems):
    copies = [
        pltpu.make_async_copy(noise_hbm.at[:, 1, :, pl.ds(t * TILE, TILE)], tiled_next.at[t], sems.at[t])
        for t in range(tiled.shape[0])
    ]
    for copy in copies:
        copy.start()
    sweep_field(0, packed, tiled, buf, work)
    for copy in copies:
        copy.wait()


def sweep_field(field, packed, tiled, buf, work):
    tiles, levels, ys, _ = tiled.shape
    columns = tiles * TILE
    ranges = TILE // levels
    span = columns // ranges
    blocks = span // TILE
    main = 16
    core = lax.axis_index("gx")
    lane = lax.broadcasted_iota(jnp.int32, (8, TILE), 1)
    keep_left = (lane >= levels) | (core == 1)
    keep_right = (lane < TILE - levels) | (core == 0)
    source = tiled.reshape(tiles, levels * ys, TILE)
    flat = buf.reshape(tiles, levels * ys, TILE)
    for slot in range(2):
        for y in range(ys):
            work[slot, y, 0:8, :] = splat(0.0)
            work[slot, y, main + span + 8 :, :] = splat(0.0)

    def pieces(y):
        return [(c, g, pl.ds(8 * g * ys + y, 8, stride=ys)) for c in range(ranges) for g in range(levels // 8)]

    for y in range(ys):
        for b in range(blocks):
            rows = [source[c * blocks + b, at, :] for c, g, at in pieces(y)]
            work[0, y, main + b * TILE : main + (b + 1) * TILE, :] = jnp.concatenate(rows, axis=0).T
        edge, place = packed[field, y // ranges], y % ranges
        left = pltpu.roll(work[0, y, main + span - 8 : main + span, :], levels, 1)
        right = pltpu.roll(work[0, y, main : main + 8, :], TILE - levels, 1)
        far_left = pltpu.roll(edge, (TILE - levels * place) % TILE, 1)
        far_right = pltpu.roll(edge, levels * (ranges - 1 - place), 1)
        left = jnp.where(keep_left, jnp.where(lane < levels, far_left, left), 0.0)
        right = jnp.where(keep_right, jnp.where(lane >= TILE - levels, far_right, right), 0.0)
        work[0, y, main - 8 : main, :] = left
        work[0, y, main + span : main + span + 8, :] = right

    def block(src, at, before, later, keep=None):
        above, here = splat(0.0), work[src, 0, at, :]
        for y in range(ys):
            below = work[src, y + 1, at, :] if y + 1 < ys else splat(0.0)
            new = here + (work[src, y, before, :] + work[src, y, later, :]) + (above + below)
            if keep is not None:
                new = jnp.where(keep, new, 0.0)
            work[1 - src, y, at, :] = new
            above, here = here, below

    for turn in range(SWEEPS):
        src = turn % 2

        def step(r, _, src=src):
            at = pl.multiple_of(main + 8 * r, 8)
            block(src, pl.ds(at, 8), pl.ds(at - 1, 8), pl.ds(at + 1, 8))
            return 0

        lax.fori_loop(0, span // 8, step, 0, unroll=True)
        if turn + 1 < SWEEPS:
            for at, keep in ((main - 8, keep_left), (main + span, keep_right)):
                block(src, pl.ds(at, 8), pl.ds(at - 1, 8), pl.ds(at + 1, 8), keep)
    for y in range(ys):
        for b in range(blocks):
            turned = work[SWEEPS % 2, y, main + b * TILE : main + (b + 1) * TILE, :].T
            for i, (c, g, at) in enumerate(pieces(y)):
                flat[c * blocks + b, at, :] = turned[8 * i : 8 * i + 8]


def filter_first(coef, mixed, after, out, buf):
    filter_field(0, coef, mixed, buf, out)


def sweep_second(packed, tiled, after, buf, work):
    sweep_field(1, packed, tiled, buf, work)


def filter_second(coef, mixed, after, out, buf):
    filter_field(1, coef, mixed, buf, out)


def filter_field(field, coef, mixed, buf, out):
    tiles, levels, ys, _ = mixed.shape
    scale = 0.2**SWEEPS
    spots = [(t, top) for t in range(tiles) for top in range(ys // 8)]

    def forward(level, state):
        alpha, gain = row(coef, 0, field, level), row(coef, 1, field, level) * scale
        new = []
        for (t, top), old in zip(spots, state):
            value = alpha * old + gain * mixed[t, level, 8 * top : 8 * top + 8, :]
            buf[t, level, 8 * top : 8 * top + 8, :] = value
            new.append(value)
        return tuple(new)

    def backward(turn, state):
        level = levels - 1 - turn
        alpha = row(coef, 0, field, level)
        gain = 1.0 - alpha
        new = []
        for (t, top), old in zip(spots, state):
            value = alpha * old + gain * buf[t, level, 8 * top : 8 * top + 8, :]
            out[level, 8 * top : 8 * top + 8, t * TILE : (t + 1) * TILE] = value
            new.append(value)
        return tuple(new)

    zeros = (splat(0.0),) * len(spots)
    lax.fori_loop(0, levels, forward, zeros, unroll=True)
    lax.fori_loop(0, levels, backward, zeros, unroll=True)


def edges(m0, m1, m2, m3, after, out):
    columns = m0.shape[2]
    near = pl.ds(pl.multiple_of((1 - lax.axis_index("gx")) * (columns - TILE), TILE), TILE)
    for k, ref in enumerate((m0, m1, m2, m3)):
        out[k] = ref[:, :, near]


def spread(m0, m1, m2, m3, after, out, work):
    columns = m0.shape[2]
    tiles = columns // TILE
    pos = position()
    for k, ref in enumerate((m0, m1, m2, m3)):
        s = pos ^ k
        for kind in range(2):
            for t in range(tiles):
                work[0, 2 * kind + s // 2, s % 2, t] = ref[kind, :, t * TILE : (t + 1) * TILE]
    for field in range(4):
        for half in range(2):
            work[0, field, half, tiles] = splat(0.0)
    diffuse(work, tiles + 1, edge_mask())
    for field in range(4):
        for half in range(2):
            for t in range(tiles):
                at = (field // 2, field % 2, slice(8 * half, 8 * half + 8), slice(t * TILE, (t + 1) * TILE))
                out[at] = work[SWEEPS % 2, field, half, t] * 0.2**SWEEPS


def finish(g0, g1, reach, bias, own, halo, latent_hbm, soft_hbm, state, work, latent, soft, sems):
    levels, columns = g0.shape[0], g0.shape[2]
    pos = position()
    keep = edge_mask()
    for k in range(GROUP):
        s = pos ^ k
        for kind in range(2):
            work[0, 2 * kind + s // 2, s % 2, 1] = halo[k, kind] * keep
            work[0, 2 * kind + s // 2, s % 2, 0] = splat(0.0)
    diffuse(work, 2, keep)
    state[...] = own[...]
    near = pl.ds(pl.multiple_of((1 - lax.axis_index("gx")) * (columns - TILE), TILE), TILE)
    for field in range(4):
        for half in range(2):
            at = (field // 2, field % 2, slice(8 * half, 8 * half + 8), near)
            state[at] += work[SWEEPS % 2, field, half, 0] * 0.2**SWEEPS
    parts = sems.shape[0]
    step = levels // parts
    tiles = columns // TILE
    copies = []
    for i in range(parts):

        def body(turn, _, i=i):
            rows = pl.ds(pl.multiple_of(8 * (turn // tiles), 8), 8)
            lanes = pl.ds(pl.multiple_of(TILE * lax.rem(turn, tiles), TILE), TILE)
            f = [state[0, field, rows, lanes] for field in range(2)]
            r = [state[1, field, rows, lanes] for field in range(2)]
            base = bias[rows, lanes]
            for level in range(i * step, (i + 1) * step):
                one = g0[level, rows, lanes] + row(reach, 0, 0, level) * f[0] + row(reach, 1, 0, level) * r[0]
                two = g1[level, rows, lanes] + row(reach, 0, 1, level) * f[1] + row(reach, 1, 1, level) * r[1]
                latent[level, 0, rows, lanes] = one
                latent[level, 1, rows, lanes] = two
                half = 0.5 + 0.5 * jnp.tanh(1.5 * (one - base))
                soft[level, rows, lanes] = half * (0.5 + 0.5 * jnp.tanh(1.5 * two))
            return 0

        lax.fori_loop(0, 2 * tiles, body, 0, unroll=True)
        at = pl.ds(i * step, step)
        copies += [
            pltpu.make_async_copy(latent.at[at], latent_hbm.at[at], sems.at[i, 0]),
            pltpu.make_async_copy(soft.at[at], soft_hbm.at[at], sems.at[i, 1]),
        ]
        for copy in copies[-2:]:
            copy.start()
    for copy in copies:
        copy.wait()


def in_hbm(value):
    return pltpu.with_memory_space_constraint(value, pltpu.HBM)


def params(mib):
    return pltpu.CompilerParams(vmem_limit_bytes=mib << 20)


def cost(flops, data):
    return pl.CostEstimate(flops=flops, bytes_accessed=data, transcendentals=0)


def xor_permute(value, axis, by):
    return lax.ppermute(value, axis, [(i, i ^ by) for i in range(lax.axis_size(axis))])


def entering_states(total, groups):
    columns = total.shape[2] - TILE
    group = lax.axis_index("gz") // GROUP

    def wide(value):
        return jnp.tile(value, (1, columns // TILE))

    def fwd(t):
        return t[0, :, :columns]

    def bwd(t):
        return t[1, :, :columns]

    if groups == 2:
        sent = jnp.where(group == 0, jnp.concatenate([total[0, :, :columns], total[0, :, columns:]], axis=1),
                         total[1])
        got = xor_permute(sent, "gz", GROUP)
        zero = jnp.zeros((8, columns), F32)
        below = got[:, :columns] + wide(got[:, columns:]) * fwd(total)
        return jnp.stack([jnp.where(group == 0, zero, got[:, :columns]), jnp.where(group == 0, below, zero)])
    size = GROUP * groups
    totals = [total]
    for turn in range(1, groups):
        totals.append(lax.ppermute(total, "gz", [(i, (i + GROUP * turn) % size) for i in range(size)]))
    stacked = jnp.stack(totals)
    state = jnp.zeros((8, columns), F32)
    f = [state]
    at = [lax.dynamic_index_in_dim(stacked, (group - j) % groups, keepdims=False) for j in range(groups)]
    for j in range(groups):
        state = wide(at[j][0, :, columns:]) * state + fwd(at[j])
        f.append(state)
    state = jnp.zeros((8, columns), F32)
    r = [None] * groups + [state]
    for j in reversed(range(groups)):
        state = bwd(at[j]) + wide(at[j][1, :, columns:]) * f[j] + wide(at[j][0, :, columns:]) * state
        r[j] = state
    return jnp.stack(
        [
            lax.dynamic_index_in_dim(jnp.stack(f[:groups]), group, keepdims=False),
            lax.dynamic_index_in_dim(jnp.stack(r[1:]), group, keepdims=False),
        ]
    )


def shards(noise, scale_index, rates, facies_code, thresholds):
    levels, _, ys, columns = noise.shape
    assert ys == 16 and levels % 8 == 0 and TILE % levels == 0 and columns * levels % (TILE * TILE) == 0
    tiles = columns // TILE
    groups = lax.axis_size("gz") // GROUP
    message = jax.ShapeDtypeStruct((2, 8, columns + TILE), F32)
    *mine, coef, packed, tiled0 = pl.pallas_call(
        carries,
        out_shape=[message] * GROUP
        + [
            jax.ShapeDtypeStruct((2, 2, levels, TILE), F32),
            jax.ShapeDtypeStruct((2, ys * levels // TILE, 8, TILE), F32),
            jax.ShapeDtypeStruct((tiles, levels, ys, TILE), F32),
        ],
        in_specs=[HBM, HBM, HBM],
        out_specs=[VMEM] * (GROUP + 3),
        scratch_shapes=[
            pltpu.VMEM((tiles, levels, ys, TILE), F32),
            pltpu.VMEM((GROUP, 2, 8, columns + TILE), F32),
            pltpu.VMEM((2, rates.shape[0], 8, TILE), F32),
            pltpu.VMEM((levels, 8, TILE), F32),
            pltpu.VMEM((2, 2, levels + 1, 8, TILE), F32),
            pltpu.SMEM((2, levels), jnp.int32),
            pltpu.SMEM(rates.shape, F32),
            pltpu.SemaphoreType.DMA((GROUP + 1, tiles)),
        ],
        compiler_params=params(50),
        cost_estimate=cost(4 * noise.size, 4 * noise.size),
        name="carries",
    )(in_hbm(scale_index.T), in_hbm(rates), in_hbm(noise))
    got = [mine[0]] + [xor_permute(mine[k], "gz", k) for k in range(1, GROUP)]
    halo = xor_permute(packed, "gx", 1)

    field_out = jax.ShapeDtypeStruct((levels, ys, columns), F32)
    field_tiled = jax.ShapeDtypeStruct((tiles, levels, ys, TILE), F32)
    scratch = [
        pltpu.VMEM((tiles, levels, ys, TILE), F32),
        pltpu.VMEM((2, ys, columns * levels // TILE + 32, TILE), F32),
    ]
    mixed, tiled1 = pl.pallas_call(
        sweep_first,
        out_shape=[field_tiled] * 2,
        in_specs=[VMEM, VMEM, HBM],
        out_specs=[VMEM] * 2,
        scratch_shapes=[scratch[1], pltpu.SemaphoreType.DMA((tiles,))],
        compiler_params=params(45),
        cost_estimate=cost(40 * noise.size, 4 * noise.size),
        name="sweep0",
    )(halo, tiled0, in_hbm(noise))
    held = pltpu.VMEM((GROUP, 2, 8, columns + TILE), F32)
    total = pl.pallas_call(
        group_total,
        out_shape=message,
        in_specs=[VMEM] * GROUP + [ANY],
        out_specs=VMEM,
        scratch_shapes=[held],
        compiler_params=params(8),
        name="group_total",
    )(*got, mixed)
    local0 = pl.pallas_call(
        filter_first,
        out_shape=field_out,
        in_specs=[VMEM, VMEM, ANY],
        out_specs=VMEM,
        scratch_shapes=[scratch[0]],
        compiler_params=params(16),
        cost_estimate=cost(8 * noise.size, noise.size),
        name="filter0",
    )(coef, mixed, total)
    reach, bias = pl.pallas_call(
        prepare,
        out_shape=[
            jax.ShapeDtypeStruct((2, 2, levels, TILE), F32),
            jax.ShapeDtypeStruct((ys, columns), F32),
        ],
        in_specs=[VMEM, VMEM, SMEM, ANY],
        out_specs=[VMEM] * 2,
        scratch_shapes=[pltpu.VMEM((levels, 8, TILE), F32)],
        compiler_params=params(4),
        cost_estimate=cost(noise.size, noise.size),
        name="prepare",
    )(coef, facies_code, thresholds, local0)
    entering = entering_states(total, groups)
    state = jax.ShapeDtypeStruct((2, 8, columns), F32)
    own = pl.pallas_call(
        enter_group,
        out_shape=[state] * GROUP,
        in_specs=[VMEM] * (GROUP + 1) + [ANY],
        out_specs=[VMEM] * GROUP,
        scratch_shapes=[held],
        compiler_params=params(8),
        name="enter_group",
    )(*got, entering, reach)
    states = [own[0]] + [xor_permute(own[k], "gz", k) for k in range(1, GROUP)]
    mixed1 = pl.pallas_call(
        sweep_second,
        out_shape=field_tiled,
        in_specs=[VMEM, VMEM, ANY],
        out_specs=VMEM,
        scratch_shapes=[scratch[1]],
        compiler_params=params(16),
        cost_estimate=cost(40 * noise.size, 4 * noise.size),
        name="sweep1",
    )(halo, tiled1, own[0])
    near = pl.pallas_call(
        edges,
        out_shape=jax.ShapeDtypeStruct((GROUP, 2, 8, TILE), F32),
        in_specs=[VMEM] * GROUP + [ANY],
        out_specs=VMEM,
        compiler_params=params(4),
        name="edges",
    )(*states, mixed1)
    spread_out = pl.pallas_call(
        spread,
        out_shape=jax.ShapeDtypeStruct((2, 2, ys, columns), F32),
        in_specs=[VMEM] * GROUP + [ANY],
        out_specs=VMEM,
        scratch_shapes=[pltpu.VMEM((2, 4, 2, tiles + 1, 8, TILE), F32)],
        compiler_params=params(8),
        cost_estimate=cost(4 * noise.size, noise.size),
        name="spread",
    )(*states, near)
    local1 = pl.pallas_call(
        filter_second,
        out_shape=field_out,
        in_specs=[VMEM, VMEM, ANY],
        out_specs=VMEM,
        scratch_shapes=[scratch[0]],
        compiler_params=params(16),
        cost_estimate=cost(8 * noise.size, noise.size),
        name="filter1",
    )(coef, mixed1, near)
    near = xor_permute(near, "gx", 1)
    out = [
        jax.ShapeDtypeStruct(noise.shape, F32),
        jax.ShapeDtypeStruct((levels, ys, columns), F32),
    ]
    latent, soft = pl.pallas_call(
        finish,
        out_shape=out,
        in_specs=[VMEM] * 6,
        out_specs=[ANY, ANY],
        scratch_shapes=[
            pltpu.VMEM((2, 2, ys, columns), F32),
            pltpu.VMEM((2, 4, 2, 2, 8, TILE), F32),
            pltpu.VMEM(noise.shape, F32),
            pltpu.VMEM((levels, ys, columns), F32),
            pltpu.SemaphoreType.DMA((8, 2)),
        ],
        compiler_params=params(24),
        name="finish",
    )(local0, local1, reach, bias, spread_out, near)
    return latent, soft


def solution(mesh):
    return jax.shard_map(
        shards,
        mesh=mesh,
        in_specs=(
            P(("parts", "gz"), None, None, "gx"),
            P(("parts", "gz"), None),
            P(),
            P("parts", "gx"),
            P(),
        ),
        out_specs=(P(("parts", "gz"), None, None, "gx"), P(("parts", "gz"), None, "gx")),
        check_vma=False,
    )
```
